32 devices in a mesh: expert: 8 (over y, x, core), dp: 4 (over z).
Axes of the slice: x: 2, y: 2, z: 4, core: 2. Of those that a mesh axis runs over, the one named last changes fastest.
Arguments:
- tokens: bfloat16 [4096, 2048], P(('expert', 'dp')), may hold values from -6 to 6
- expert_ids: int32 [4096, 4], P(('expert', 'dp')), may hold values from 0 to 15, all different within a row; in each aligned block of 128 rows (0 to 127, 128 to 255, ...) at most 96 rows name the same one
- gate_probs: float32 [4096, 4], P(('expert', 'dp')), may hold values from 0.05 to 0.5
- expert_weights: bfloat16 [2048, 3, 16, 384], P(None, None, 'expert'), may hold values from -0.125 to 0.125
- out_grad: bfloat16 [4096, 2048], P(('expert', 'dp')), may hold values from -1.5 to 1.5
Outputs:
- layer_out: bfloat16 [4096, 2048], P(('expert', 'dp'))
- token_grad: bfloat16 [4096, 2048], P(('expert', 'dp'))
- gate_grad: float32 [4096, 4], P(('expert', 'dp'))
- weight_grad: float32 [2048, 3, 16, 384], P('dp', None, 'expert')
The draws below stay inside these ranges and needn't reach their ends.
Inputs may be any that keep to these rules, and one draw needn't show every extreme that they name: `expert_ids`: each row names 4 different experts. Among the 128 rows of one device (aligned blocks of rows), no expert is named by more than 96 rows, and in some block some expert is named by exactly 96 rows.
All inputs are finite; a program needn't handle non-finite values.
Results may differ from the reference program's by a relative error of at most 0.0085.
Values may be sent and summed in bfloat16 or wider, within the bound.
A program may use at most 128 MiB of HBM per device.

```python
import math
import jax
import jax.numpy as jnp
import numpy as np
from jax import lax

D = 2048
H = 384
TOP = 4
TOK_DEV = 128
EXPERTS = 16
CAP = 96
TOKENS = 4096
N_DP = 4


def spiked(values, own_key, source, target, parts, factor):
    owner, partner = [(jnp.arange(values.shape[dim]) // (values.shape[dim] // parts)).reshape([-1 if axis == dim else 1 for axis in range(values.ndim)]) for dim in (source, target)]
    chosen = jax.random.permutation(own_key, parts)[partner]
    strong = (owner == chosen) | (owner == (partner + parts // 2) % parts)
    return jnp.where(strong, factor * values, values)


def block_scale(stream_key, shape, pieces, least, largest):
    def one(dim, parts):
        draws = jax.random.uniform(jax.random.fold_in(jax.random.fold_in(stream_key, 6), dim), (parts,), jnp.float32, least / len(pieces), largest / len(pieces))
        return jnp.repeat(jnp.exp(draws), shape[dim] // parts).reshape((-1,) + (1,) * (len(shape) - dim - 1))

    level = one(*pieces[0])
    for cut in pieces[1:]:
        level = level * one(*cut)
    return level


def assign_block(rng, own, number, rows, number_of, top, limit, lean):
    order = jax.random.permutation(rng, number_of)
    crowded, usual = shares(number_of, rows * top, limit, lean, True), shares(number_of, rows * top, limit, lean, False)
    places = jnp.arange(number_of)

    def named(tallies, rotation):
        used = int((tallies > 0).sum())
        fixed = max(1, used // 4)
        passed = fixed + (places - fixed + rotation * (used - fixed)) % max(1, number_of - fixed)
        return jnp.zeros((number_of,), jnp.int32).at[order[jnp.where(places < fixed, places, passed)]].set(jnp.asarray(tallies, jnp.int32))

    tallies = jnp.where(number % 4 == 0, named(crowded, number // 4), named(usual, number - number // 4 - 1))
    mixed = jax.random.permutation(jax.random.fold_in(own, 3), number_of)
    source_of, receiver = mixed[0:number_of // 2 * 2:2], mixed[1:number_of // 2 * 2:2]
    slack = jnp.minimum(tallies[source_of] - 1, limit - tallies[receiver]) // 2
    slack = jnp.where((source_of == order[0]) | (receiver == order[0]) | (tallies[receiver] == 0), 0, jnp.maximum(slack, 0))
    passed = jax.random.randint(jax.random.fold_in(own, 4), (number_of // 2,), 0, 1 << 20) % (slack + 1)
    tallies = tallies.at[source_of].add(-passed).at[receiver].add(passed)
    labels = jnp.searchsorted(jnp.cumsum(tallies), jnp.arange(rows * top), side="right").astype(jnp.int32)
    grid = labels.reshape(top, rows).T
    grid = grid[jax.random.permutation(jax.random.fold_in(own, 1), rows)]
    rotation = jax.random.randint(jax.random.fold_in(own, 2), (rows, 1), 0, top)
    return jnp.take_along_axis(grid, (jnp.arange(top)[None, :] + rotation) % top, axis=1)


def shares(number_of, total, bound, lean, full):
    weights = [(1 << 20) // math.isqrt(rank ** lean) + 1 for rank in range(1, number_of + 1)]
    largest = bound if full else min(bound, max(-(-total // number_of), total * weights[0] // sum(weights)))
    least = 1 if total - largest >= number_of - 1 else 0
    counts, rest = [largest] + [least] * (number_of - 1), total - largest - least * (number_of - 1)
    while rest > 0:
        free = [i for i in range(1, number_of) if counts[i] < largest] or [i for i in range(1, number_of) if counts[i] < bound]
        pool, left = sum([weights[i] for i in free]), rest
        for i in free:
            more = min(bound - counts[i], max(1, left * weights[i] // pool), rest)
            counts[i] = counts[i] + more
            rest = rest - more
    return np.array(counts)


def scatter_about(stream_key, dims, scale, most, cuts=(), kind=jnp.bfloat16):
    gain = block_scale(stream_key, dims, cuts, -0.22, 0.18) if cuts else 1.0
    values = jax.random.normal(stream_key, dims, jnp.float32) * scale * gain
    return jnp.minimum(jnp.maximum(values, -most), most).astype(kind)


def heavy_noise(rng, dims, width, limit, pieces, heavy, held_as=jnp.bfloat16):
    entries = width * jax.random.normal(rng, dims, jnp.float32)
    if pieces:
        entries = entries * block_scale(rng, dims, pieces, -0.22, 0.18)
    return jnp.clip(spiked(entries, jax.random.fold_in(rng, 3), *heavy), -limit, limit).astype(held_as)


def setup_inputs(seed: int = 0) -> dict:
    streams_of = jax.random.split(jax.random.key(seed), 6)
    tokens = heavy_noise(streams_of[0], (TOKENS, D), 1.0, 6.0, ((0, 32),), (0, 1, 32, 2.75))
    expert_ids_keys = jax.random.split(jax.random.fold_in(streams_of[1], 1), TOKENS // TOK_DEV)
    expert_ids_turns = jax.random.permutation(jax.random.fold_in(streams_of[1], 3), TOKENS // TOK_DEV)
    expert_ids = jax.vmap(lambda own, number: assign_block(jax.random.fold_in(streams_of[1], 2), own, number, TOK_DEV, EXPERTS, TOP, CAP, 2))(expert_ids_keys, expert_ids_turns).reshape((TOKENS, TOP))
    gate_probs = jnp.clip(0.05 + 0.45 * jax.random.uniform(streams_of[2], (TOKENS, TOP), jnp.float32) ** block_scale(streams_of[2], (TOKENS, TOP), ((0, 32),), -0.2, 0.2), 0.05, 0.5)
    expert_weights = scatter_about(streams_of[3], (D, 3, EXPERTS, H), D ** -0.5, 0.125, ((2, 8),))
    out_grad = scatter_about(streams_of[4], (TOKENS, D), 0.25, 1.5, ((0, 32),))
    return dict(tokens=tokens, expert_ids=expert_ids, gate_probs=gate_probs, expert_weights=expert_weights, out_grad=out_grad)


def rounded(values):
    return lax.optimization_barrier(values.astype(jnp.bfloat16)).astype(jnp.float32)


def reference(tokens, expert_ids, gate_probs, expert_weights, out_grad):
    tile_rows = 128
    pair_count = TOKENS * TOP
    key_count = EXPERTS * N_DP
    tile_count = pair_count // tile_rows + key_count
    pair_index = jnp.arange(pair_count, dtype=jnp.int32)
    pair_token = (pair_index // TOP).astype(jnp.int32)
    pair_expert = expert_ids.reshape(pair_count).astype(jnp.int32)
    pair_group = ((pair_token // TOK_DEV) % N_DP).astype(jnp.int32)
    pair_key = (pair_expert * N_DP + pair_group).astype(jnp.int32)
    key_sizes = jnp.zeros((key_count,), jnp.int32).at[pair_key].add(1)
    key_tiles = ((key_sizes + tile_rows - 1) // tile_rows).astype(jnp.int32)
    tile_first = (jnp.cumsum(key_tiles) - key_tiles).astype(jnp.int32)
    key_first = (jnp.cumsum(key_sizes) - key_sizes).astype(jnp.int32)
    ordering = jnp.argsort(pair_key, stable=True).astype(jnp.int32)
    sorted_key = pair_key[ordering]
    position = (tile_first[sorted_key] * tile_rows + pair_index - key_first[sorted_key]).astype(jnp.int32)
    slot_pair = jnp.full((tile_count * tile_rows,), -1, jnp.int32).at[position].set(ordering)
    tile_key = (jnp.searchsorted(tile_first, jnp.arange(tile_count, dtype=jnp.int32), side="right") - 1).astype(jnp.int32)
    flat_probs = gate_probs.reshape(pair_count)

    def step(carry, inputs):
        layer_acc, token_acc, gate_acc, group_acc, weight_acc, prev_key = carry
        slots, key_now = inputs
        filled = slots >= 0
        safe_pair = jnp.maximum(slots, 0)
        token_row = (safe_pair // TOP).astype(jnp.int32)
        expert_now = (key_now // N_DP).astype(jnp.int32)
        weight_now = lax.dynamic_index_in_dim(expert_weights, expert_now, axis=2, keepdims=False)
        row_block = jnp.where(filled[:, None], tokens[token_row], jnp.zeros((), jnp.bfloat16))
        gate_pre = jnp.dot(row_block, weight_now[:, 0], preferred_element_type=jnp.float32)
        up_pre = jnp.dot(row_block, weight_now[:, 1], preferred_element_type=jnp.float32)
        sigmoid_gate = jax.nn.sigmoid(gate_pre)
        hidden = (gate_pre * sigmoid_gate * up_pre).astype(jnp.bfloat16)
        output = jnp.dot(hidden, weight_now[:, 2].T, preferred_element_type=jnp.float32).astype(jnp.bfloat16)
        probs = jnp.where(filled, flat_probs[safe_pair], jnp.zeros((), jnp.float32))
        grad_block = out_grad[token_row]
        dump_token = jnp.where(filled, token_row, TOKENS)
        dump_pair = jnp.where(filled, safe_pair, pair_count)
        layer_acc = layer_acc.at[dump_token].add(probs[:, None] * output.astype(jnp.float32), mode="drop")
        gate_term = jnp.sum(grad_block.astype(jnp.float32) * output.astype(jnp.float32), axis=1)
        gate_acc = gate_acc.at[dump_pair].add(gate_term, mode="drop")
        out_cot = (probs[:, None] * grad_block.astype(jnp.float32)).astype(jnp.bfloat16)
        hidden_cot = jnp.dot(out_cot, weight_now[:, 2], preferred_element_type=jnp.float32)
        gate_cot = (hidden_cot * up_pre * sigmoid_gate * (1.0 + gate_pre * (1.0 - sigmoid_gate))).astype(jnp.bfloat16)
        up_cot = (hidden_cot * (gate_pre * sigmoid_gate)).astype(jnp.bfloat16)
        token_cot = (jnp.dot(gate_cot, weight_now[:, 0].T, preferred_element_type=jnp.float32)
                     + jnp.dot(up_cot, weight_now[:, 1].T, preferred_element_type=jnp.float32)).astype(jnp.bfloat16)
        token_acc = token_acc.at[dump_token].add(token_cot.astype(jnp.float32), mode="drop")
        tile_grad = jnp.stack([
            jnp.dot(row_block.T, gate_cot, preferred_element_type=jnp.float32),
            jnp.dot(row_block.T, up_cot, preferred_element_type=jnp.float32),
            jnp.dot(out_cot.T, hidden, preferred_element_type=jnp.float32)], axis=1)
        changed = key_now != prev_key
        prev_expert = (jnp.maximum(prev_key, 0) // N_DP).astype(jnp.int32)
        flushed = jnp.where(changed & (prev_key >= 0), rounded(group_acc), jnp.zeros((), jnp.float32))
        weight_acc = weight_acc.at[:, :, prev_expert].add(flushed)
        group_acc = jnp.where(changed, jnp.zeros((), jnp.float32), group_acc) + tile_grad
        return (layer_acc, token_acc, gate_acc, group_acc, weight_acc, key_now), None

    start = (jnp.zeros((TOKENS, D), jnp.float32), jnp.zeros((TOKENS, D), jnp.float32),
             jnp.zeros((pair_count,), jnp.float32), jnp.zeros((D, 3, H), jnp.float32),
             jnp.zeros((D, 3, EXPERTS, H), jnp.float32), jnp.array(-1, jnp.int32))
    final, unused = lax.scan(step, start, (slot_pair.reshape(tile_count, tile_rows), tile_key))
    layer_acc, token_acc, gate_acc, group_acc, weight_acc, prev_key = final
    last_expert = (jnp.maximum(prev_key, 0) // N_DP).astype(jnp.int32)
    weight_acc = weight_acc.at[:, :, last_expert].add(rounded(group_acc))
    return (layer_acc.astype(jnp.bfloat16), token_acc.astype(jnp.bfloat16),
            gate_acc.reshape(TOKENS, TOP), weight_acc)
```

```python
import functools
import jax
import jax.numpy as jnp
from jax import lax
from jax.experimental import pallas as pl
from jax.experimental.pallas import tpu as pltpu
from jax.sharding import Mesh, PartitionSpec as P

F32 = jnp.float32
BF16 = jnp.bfloat16
SWAP = [(0, 1), (1, 0)]
EXTRA = 16


def dot(a, b, ca, cb):
    return lax.dot_general(a, b, (((ca,), (cb,)), ((), ())), preferred_element_type=F32)


def fused_kernel(
    tok_ref, og_ref, meta_ref, w_ref,
    lay_ref, tg_ref, gg_ref, wg_ref, buf,
    wv, xg, act, po, ps, pr, rx, ggs,
    loc_sem, w_sem, ld_sem,
    xy_s, xy_r, za_s, za_r, zb_s, zb_r, sib_s, sib_r,
    ps_s, ps_r, rx_s, rx_r, gg_s, gg_r,
):
    tok, d = tok_ref.shape
    rows = 2 * tok + EXTRA
    hh = w_ref.shape[1] // 3
    h = hh // 2
    ch = d // 4
    nt = min(256, hh)
    dt = min(512, d)
    me = lax.axis_index("expert")
    z = lax.axis_index("dp")
    core = me % 2
    xx = (me // 2) % 2
    yy = me // 4

    def peer(m, r):
        return (
            ((yy + m // 2) % 2) * 4 + ((xx + m % 2) % 2) * 2 + (core + r) % 2,
            z,
        )

    xn, yn, sib = peer(1, 0), peer(2, 0), peer(0, 1)
    order = [z, 1 + z % 2, (2 + 3 * z) % 5, 3 - 3 * (z // 2)]

    own_half = tok // 16 * 16 + 0 * EXTRA
    cut_a = (rows * 11 // 16 + 8) // 16 * 16
    a_half = (cut_a // 2 + 8) // 16 * 16
    h1, h2 = (0, own_half), (own_half, rows - own_half)
    a1, a2 = (0, a_half), (a_half, cut_a - a_half)
    whole, pa, pb = (0, rows), (0, cut_a), (cut_a, rows - cut_a)

    def rdma(src, dst, ssem, rsem, dev):
        return pltpu.make_async_remote_copy(
            src_ref=src, dst_ref=dst, send_sem=ssem, recv_sem=rsem,
            device_id=dev, device_id_type=pl.DeviceIdType.MESH,
        )

    def at(r, k, m, part):
        return buf.at[r, k, m, pl.ds(part[0], part[1])]

    def xy(k, i, own):
        p1, p2 = (h1, h2) if own else (a1, a2)
        src, dst, part, dev = [
            (0, 1, p1, xn), (0, 1, p2, xn), (0, 2, p2, yn), (0, 2, p1, yn),
            (1, 3, p1, yn), (2, 3, p2, xn),
        ][i]
        return rdma(at(0, k, src, part), at(0, k, dst, part), xy_s.at[k, i], xy_r.at[k, i], dev)

    def line(k, m, up):
        dev = (me, z + 1) if up else (me, z - 1)
        u = 1 if up else 0
        if m is None:
            return rdma(at(0, k, 0, pa), at(0, k, 0, pa), za_s.at[k, u], za_r.at[k], dev)
        return rdma(at(0, k, m, pb), at(0, k, m, pb), zb_s.at[k, m, u], zb_r.at[k, m], dev)

    def on_line(k, m, what):
        @pl.when((k <= z) & (z < 3))
        def _():
            getattr(line(k, m, True), what)()

        @pl.when((k >= z) & (z > 0))
        def _():
            getattr(line(k, m, False), what)()

    def sibling(k, m, i, part):
        return rdma(at(0, k, m, part), at(1, k, m, part), sib_s.at[k, m, i], sib_r.at[k, m, i], sib)

    own = [
        pltpu.make_async_copy(tok_ref, at(0, z, 0, (0, tok)), loc_sem.at[0]),
        pltpu.make_async_copy(og_ref, at(0, z, 0, (tok, tok)), loc_sem.at[1]),
        pltpu.make_async_copy(meta_ref, at(0, z, 0, (2 * tok, EXTRA)), loc_sem.at[2]),
    ]
    wcopy = pltpu.make_async_copy(w_ref, wv, w_sem)
    for c in own:
        c.start()
    barrier = pltpu.get_barrier_semaphore()
    for i in range(1, 8):
        pl.semaphore_signal(barrier, inc=1, device_id=peer(i // 2, i % 2), device_id_type=pl.DeviceIdType.MESH)

    @pl.when(z > 0)
    def _():
        pl.semaphore_signal(barrier, inc=1, device_id=(me, z - 1), device_id_type=pl.DeviceIdType.MESH)

    @pl.when(z < 3)
    def _():
        pl.semaphore_signal(barrier, inc=1, device_id=(me, z + 1), device_id_type=pl.DeviceIdType.MESH)

    pl.semaphore_wait(barrier, 8 + (z + 1) // 2 % 2)

    for c in own:
        c.wait()
    for i in (0, 2):
        xy(z, i, True).start()
    on_line(z, None, "start")
    for i in (1, 3):
        xy(z, i, True).start()
    sibling(z, 0, 0, whole).start()
    on_line(z, 0, "start")
    wcopy.start()
    wg_ref[...] = jnp.zeros_like(wg_ref)

    def own_stage():
        xy(z, 0, True).wait_recv()
        xy(z, 4, True).start()
        xy(z, 2, True).wait_recv()
        xy(z, 5, True).start()
        xy(z, 1, True).wait_recv()
        on_line(z, 1, "start")
        sibling(z, 1, 0, whole).start()
        xy(z, 3, True).wait_recv()
        on_line(z, 2, "start")
        sibling(z, 2, 0, whole).start()

    def own_stage2():
        xy(z, 4, True).wait_recv()
        xy(z, 5, True).wait_recv()
        on_line(z, 3, "start")
        sibling(z, 3, 0, whole).start()

    def far_a(k):
        line(k, None, True).wait_recv()
        for i in range(4):
            xy(k, (0, 2, 1, 3)[i], False).start()
        on_line(k, None, "start")
        sibling(k, 0, 0, pa).start()

    def far_b(k, m):
        line(k, m, True).wait_recv()
        on_line(k, m, "start")
        sibling(k, m, 1, pb).start()

    def far_fwd(k):
        xy(k, 0, False).wait_recv()
        xy(k, 4, False).start()
        xy(k, 2, False).wait_recv()
        xy(k, 5, False).start()

    def far_in(k):
        xy(k, 1, False).wait_recv()
        sibling(k, 1, 0, pa).start()
        xy(k, 3, False).wait_recv()
        sibling(k, 2, 0, pa).start()

    def far_in2(k):
        xy(k, 4, False).wait_recv()
        xy(k, 5, False).wait_recv()
        sibling(k, 3, 0, pa).start()

    def load(k, s, slot, what):
        for mi in range(2):
            for r in range(2):
                b = mi * 2 + r
                getattr(
                    pltpu.make_async_copy(buf.at[r, k, 2 * s + mi], xg.at[slot, b], ld_sem.at[slot, b]), what
                )()

    def arrived(k, s, mine):
        for m in (2 * s, 2 * s + 1):
            if mine:
                sibling(k, m, 0, whole).wait_recv()
            else:
                sibling(k, m, 0, pa).wait_recv()
                sibling(k, m, 1, pb).wait_recv()

    def first(slot, s, mine):
        def tile(n, gg):
            c0 = pl.multiple_of(n * nt, nt)
            xs = xg[slot, :, 0:tok, :].reshape(4 * tok, d)
            gs = xg[slot, :, tok : 2 * tok, :].reshape(4 * tok, d)
            gate = dot(xs, wv[:, pl.ds(c0, nt)], 1, 0)
            up = dot(xs, wv[:, pl.ds(hh + c0, nt)], 1, 0)
            u = dot(gs, wv[:, pl.ds(2 * hh + c0, nt)], 1, 0)
            col = c0 + lax.broadcasted_iota(jnp.int32, (2 * EXTRA, nt), 1)
            row = lax.broadcasted_iota(jnp.int32, (2 * EXTRA, nt), 0) % EXTRA
            sel = (row == 2 * me + (col >= h).astype(jnp.int32)).astype(F32).astype(BF16)
            ps_ = []
            for b in range(4):
                both = jnp.concatenate(
                    [xg[slot, b, 2 * tok :, 0:tok], xg[slot, b, 2 * tok :, tok : 2 * tok]], axis=0
                )
                ps_.append(dot(both, sel, 0, 0))
            p = jnp.concatenate(ps_, axis=0)
            s_ = jax.nn.sigmoid(gate)
            act_ = gate * s_
            hidden = act_ * up
            hc = p * u
            act[:, pl.ds(c0, nt)] = (hc * up * (s_ + act_ * (1.0 - s_))).astype(BF16)
            act[:, pl.ds(hh + c0, nt)] = (hc * act_).astype(BF16)
            act[:, pl.ds(2 * hh + c0, nt)] = (p * hidden).astype(BF16)
            if mine:
                uh = u * hidden
                hi = uh.astype(BF16)
                lo = (uh - hi.astype(F32)).astype(BF16)
                own_row = lax.broadcasted_iota(jnp.int32, (8, nt), 0)
                own_col = c0 + lax.broadcasted_iota(jnp.int32, (8, nt), 1)
                pick = (own_row == (own_col >= h).astype(jnp.int32)).astype(F32).astype(BF16)
                gg = gg + dot(pick, hi, 1, 1) + dot(pick, lo, 1, 1)
            return gg

        start = jnp.zeros((8, 4 * tok), F32)
        gg = lax.fori_loop(0, hh // nt, tile, start)
        if mine:
            for b in range(4):
                ggs[4 * s + b] = gg[:, b * tok : (b + 1) * tok]

    def third(slot):
        x0 = pl.multiple_of(z * ch, ch)
        xs = xg[slot, :, 0:tok, pl.ds(x0, ch)].reshape(4 * tok, ch)
        wg_ref[:, 0 : 2 * hh] += dot(xs, act[:, 0 : 2 * hh], 0, 0)
        gs = xg[slot, :, tok : 2 * tok, pl.ds(x0, ch)].reshape(4 * tok, ch)
        wg_ref[:, 2 * hh :] += dot(gs, act[:, 2 * hh :], 0, 0)

    def second(s):
        def tile(n, carry):
            r0 = pl.multiple_of(n * dt, dt)
            out = dot(act[:, 2 * hh :], wv[pl.ds(r0, dt), 2 * hh :], 1, 1).astype(BF16)
            tg = dot(act[:, : 2 * hh], wv[pl.ds(r0, dt), : 2 * hh], 1, 1).astype(BF16)
            for mi in range(2):
                for q, v in ((0, out), (1, tg)):
                    b = 2 * mi * tok
                    po[q, 2 * s + mi, :, pl.ds(r0, dt)] = v[b : b + tok]
                    ps[q, 2 * s + mi, :, pl.ds(r0, dt)] = v[b + tok : b + 2 * tok]
            return carry

        lax.fori_loop(0, d // dt, tile, 0)

    def swap(q, s):
        part = pl.ds(2 * s, 2)
        return rdma(ps.at[q, part], pr.at[q, part], ps_s.at[q, s], ps_r.at[q, s], sib)

    def add(i, j):
        po[i] = (po[i].astype(F32) + j.astype(F32)).astype(BF16)

    def merge(q, s):
        swap(q, s).wait_recv()
        for m in (2 * s, 2 * s + 1):
            add((q, m), pr[q, m])

    def back(q, i):
        near, far = (1, 2) if q == 0 else (2, 1)
        dev, dev2 = (xn, yn) if q == 0 else (yn, xn)
        if i < 2:
            return rdma(po.at[q, (near, 3)[i]], rx.at[q, i], rx_s.at[q, i], rx_r.at[q, i], dev)
        return rdma(po.at[q, far], rx.at[q, 2], rx_s.at[q, 2], rx_r.at[q, 2], dev2)

    def back_mid(q):
        far = 2 if q == 0 else 1
        back(q, 1).wait_recv()
        add((q, far), rx[q, 1])
        back(q, 2).start()

    def back_end(q, ref):
        back(q, 0).wait_recv()
        back(q, 2).wait_recv()
        ref[...] = (po[q, 0].astype(F32) + rx[q, 0].astype(F32) + rx[q, 2].astype(F32)).astype(BF16)

    def gg_copy(i):
        return rdma(ggs.at[i], gg_ref.at[i], gg_s.at[i], gg_r.at[i], peer(i // 2, i % 2))

    own_stage()
    wcopy.wait()
    arrived(z, 0, True)
    load(z, 0, 0, "start")
    own_stage2()
    k1, k2, k3 = order[1:]
    load(z, 0, 0, "wait")
    arrived(z, 1, True)
    load(z, 1, 1, "start")
    first(0, 0, True)
    far_a(k1)
    second(0)
    for q in range(2):
        swap(q, 0).start()
    for m in range(2):
        far_b(k1, m)
    third(0)
    load(z, 1, 1, "wait")
    first(1, 1, True)
    far_fwd(k1)
    second(1)
    for q in range(2):
        swap(q, 1).start()
    for i in range(1, 8):
        gg_copy(i).start()
    gg_ref[0] = ggs[0]
    merge(0, 0)
    merge(1, 0)
    far_in(k1)
    for m in range(2, 4):
        far_b(k1, m)
    merge(0, 1)
    merge(1, 1)
    for q in range(2):
        back(q, 1).start()
        back(q, 0).start()
    third(1)
    far_in2(k1)
    far_a(k2)
    arrived(k1, 0, False)
    load(k1, 0, 0, "start")
    arrived(k1, 1, False)
    load(k1, 1, 1, "start")
    load(k1, 0, 0, "wait")
    first(0, 0, False)
    back_mid(0)
    back_mid(1)
    far_fwd(k2)
    third(0)
    far_b(k2, 0)
    far_b(k2, 1)
    load(k1, 1, 1, "wait")
    first(1, 1, False)
    far_in(k2)
    far_b(k2, 2)
    far_b(k2, 3)
    third(1)
    far_in2(k2)
    far_a(k3)
    arrived(k2, 0, False)
    load(k2, 0, 0, "start")
    arrived(k2, 1, False)
    load(k2, 1, 1, "start")
    load(k2, 0, 0, "wait")
    first(0, 0, False)
    far_fwd(k3)
    back_end(0, lay_ref)
    back_end(1, tg_ref)
    third(0)
    far_b(k3, 0)
    far_b(k3, 1)
    load(k2, 1, 1, "wait")
    first(1, 1, False)
    third(1)
    far_in(k3)
    arrived(k3, 0, False)
    load(k3, 0, 0, "start")
    far_b(k3, 2)
    far_b(k3, 3)
    far_in2(k3)
    load(k3, 0, 0, "wait")
    first(0, 0, False)
    arrived(k3, 1, False)
    load(k3, 1, 1, "start")
    third(0)
    load(k3, 1, 1, "wait")
    first(1, 1, False)
    third(1)

    for i in range(6):
        xy(z, i, True).wait_send()
    for m in range(4):
        sibling(z, m, 0, whole).wait_send()
    for k in (k1, k2, k3):
        for i in range(6):
            xy(k, i, False).wait_send()
        for m in range(4):
            sibling(k, m, 0, pa).wait_send()
            sibling(k, m, 1, pb).wait_send()
    for k in order:
        on_line(k, None, "wait_send")
        for m in range(4):
            on_line(k, m, "wait_send")
    for q in range(2):
        for s in range(2):
            swap(q, s).wait_send()
        for i in range(3):
            back(q, i).wait_send()
    for i in range(1, 8):
        gg_copy(i).wait_recv()
        gg_copy(i).wait_send()


def fused(tokens, expert_ids, gate_probs, expert_weights, out_grad):
    tok, top = expert_ids.shape
    d = tokens.shape[1]
    local_experts, h = expert_weights.shape[2:]
    hh = local_experts * h
    experts = 8 * local_experts
    rows = 2 * tok + EXTRA
    me = lax.axis_index("expert")

    hot = expert_ids[:, :, None] == jnp.arange(experts)
    p = jnp.sum(jnp.where(hot, gate_probs[:, :, None], 0.0), axis=1).T
    hi = lax.reduce_precision(p, 8, 7)
    meta = jnp.concatenate(
        [hi, p - hi, jnp.zeros((experts, d - 2 * tok), F32)], axis=1
    ).astype(BF16)
    w = expert_weights.reshape(d, 3 * hh)

    any_ = pl.BlockSpec(memory_space=pl.ANY)
    vmem = pl.BlockSpec(memory_space=pltpu.VMEM)
    dma = pltpu.SemaphoreType.DMA
    lay, tg, gg, wg, _ = pl.pallas_call(
        fused_kernel,
        out_shape=[
            jax.ShapeDtypeStruct((tok, d), BF16),
            jax.ShapeDtypeStruct((tok, d), BF16),
            jax.ShapeDtypeStruct((8, 8, tok), F32),
            jax.ShapeDtypeStruct((d // 4, 3 * hh), F32),
            jax.ShapeDtypeStruct((2, 4, 4, rows, d), BF16),
        ],
        in_specs=[any_] * 4,
        out_specs=[vmem, vmem, vmem, vmem, any_],
        scratch_shapes=[
            pltpu.VMEM((d, 3 * hh), BF16),
            pltpu.VMEM((2, 4, rows, d), BF16),
            pltpu.VMEM((4 * tok, 3 * hh), BF16),
            pltpu.VMEM((2, 4, tok, d), BF16),
            pltpu.VMEM((2, 4, tok, d), BF16),
            pltpu.VMEM((2, 4, tok, d), BF16),
            pltpu.VMEM((2, 3, tok, d), BF16),
            pltpu.VMEM((8, 8, tok), F32),
            dma((3,)), dma, dma((2, 4)),
            dma((4, 6)), dma((4, 6)), dma((4, 2)), dma((4,)),
            dma((4, 4, 2)), dma((4, 4)), dma((4, 4, 2)), dma((4, 4, 2)),
            dma((2, 2)), dma((2, 2)), dma((2, 3)), dma((2, 3)), dma((8,)), dma((8,)),
        ],
        compiler_params=pltpu.CompilerParams(
            collective_id=0, has_side_effects=True, vmem_limit_bytes=60 * 1024 * 1024
        ),
    )(tokens, out_grad, meta, w)

    rel = jnp.arange(8)
    source = (
        (me // 4 + rel // 4) % 2 * 4 + (me // 2 + rel // 2) % 2 * 2 + (me + rel) % 2
    )
    named = source[:, None] * local_experts + jnp.arange(local_experts)
    match = expert_ids[:, :, None, None] == named
    value = jnp.transpose(gg[:, :local_experts], (2, 0, 1))[:, None]
    gate_grad = jnp.sum(jnp.where(match, value, 0.0), axis=(2, 3))
    return lay, tg, gate_grad, wg.reshape(d // 4, 3, local_experts, h)


def gather(rows):
    n = lax.axis_size("chip")
    own = [rows] + [
        lax.ppermute(rows, "chip", [(i, i ^ k) for i in range(n)]) for k in range(1, n)
    ]
    own = jnp.concatenate(own, axis=0)
    return jnp.concatenate([own, lax.ppermute(own, "core", SWAP)], axis=0)


def scatter(own, other):
    n = lax.axis_size("chip")
    me = lax.axis_index("chip")
    total = own + lax.ppermute(other, "core", SWAP).astype(F32)
    total = total.astype(other.dtype).reshape((n, -1) + own.shape[1:])
    total = jnp.concatenate(
        [lax.dynamic_index_in_dim(total, me ^ k, 0, keepdims=False) for k in range(n)],
        axis=0,
    )
    return lax.psum_scatter(total, "chip", scatter_dimension=0, tiled=True)


def line_scatter(grad):
    n = lax.axis_size("dp")
    me = lax.axis_index("dp")
    rows = grad.shape[0] // n

    def chunk(i):
        i = jnp.clip(i, 0, n - 1)
        return lax.dynamic_slice_in_dim(grad, i * rows, rows, 0).astype(F32)

    up = down = None
    for t in range(n - 1):
        a = chunk(n - 1 - t + me)
        b = chunk(t - (n - 1) + me)
        if t:
            a = a + up.astype(F32)
            b = b + down.astype(F32)
        up = lax.ppermute(a.astype(BF16), "dp", [(i, i + 1) for i in range(t + 1)])
        down = lax.ppermute(
            b.astype(BF16), "dp", [(i, i - 1) for i in range(n - 1 - t, n)]
        )
    return chunk(me) + up.astype(F32) + down.astype(F32)


def local(tokens, expert_ids, gate_probs, expert_weights, out_grad):
    tok_count, top_count = expert_ids.shape
    d = tokens.shape[1]
    chips = lax.axis_size("chip")
    me = lax.axis_index("chip") * 2 + lax.axis_index("core")
    local_experts, h = expert_weights.shape[2:]
    half = chips * tok_count
    eh = local_experts * h

    x = gather(tokens)
    small = gather(jnp.concatenate([expert_ids.astype(F32), gate_probs], axis=1))
    g = gather(out_grad)
    ids = small[:, :top_count].astype(jnp.int32)
    probs = small[:, top_count:]

    hits = [ids == me * local_experts + i for i in range(local_experts)]
    p = jnp.concatenate(
        [
            jnp.broadcast_to(
                jnp.sum(jnp.where(hit, probs, 0.0), axis=1, keepdims=True), (2 * half, h)
            )
            for hit in hits
        ],
        axis=1,
    )

    w = expert_weights.reshape(d, 3 * eh)
    wgu = w[:, : 2 * eh]
    wd = w[:, 2 * eh :]

    a = dot(x, wgu, 1, 0)
    gate = a[:, :eh]
    up = a[:, eh:]
    s = jax.nn.sigmoid(gate)
    hidden = gate * s * up
    ph = (p * hidden).astype(BF16)
    down_grad = line_scatter(dot(g, ph, 0, 0).astype(BF16))

    u = dot(g, wd, 1, 0)
    hc = p * u
    gc = (hc * up * s * (1.0 + gate * (1.0 - s))).astype(BF16)
    uc = (hc * gate * s).astype(BF16)
    gate_part = line_scatter(dot(x, gc, 0, 0).astype(BF16))
    up_part = line_scatter(dot(x, uc, 0, 0).astype(BF16))

    other = dot(ph[half:], wd, 1, 1).astype(BF16)
    layer_out = scatter(dot(ph[:half], wd, 1, 1), other)

    cots = jnp.concatenate([gc, uc], axis=1)
    other = dot(cots[half:], wgu, 1, 1).astype(BF16)
    token_grad = scatter(dot(cots[:half], wgu, 1, 1), other)

    uh = u * hidden
    ggk = sum(
        jnp.where(hit, jnp.sum(uh[:, i * h : (i + 1) * h], axis=1, keepdims=True), 0.0)
        for i, hit in enumerate(hits)
    )
    gate_grad = scatter(ggk[:half], ggk[half:])

    weight_grad = jnp.stack([gate_part, up_part, down_grad], axis=1)
    weight_grad = weight_grad.reshape(-1, 3, local_experts, h)
    return (layer_out, token_grad, gate_grad, weight_grad)


def solution(mesh):
    experts, groups = mesh.devices.shape
    if (experts, groups) == (8, 4):
        tok = P(("expert", "dp"), None)
        return jax.shard_map(
            fused,
            mesh=mesh,
            in_specs=(tok, tok, tok, P(None, None, "expert", None), tok),
            out_specs=(tok, tok, tok, P("dp", None, "expert", None)),
            check_vma=False,
        )
    split = Mesh(
        mesh.devices.reshape(experts // 2, 2, groups), ("chip", "core", "dp")
    )
    tok = P(("chip", "core", "dp"), None)
    wsp = P(None, None, ("chip", "core"), None)
    return jax.shard_map(
        local,
        mesh=split,
        in_specs=(tok, tok, tok, wsp, tok),
        out_specs=(tok, tok, tok, P("dp", None, ("chip", "core"), None)),
        check_vma=False,
    )
```

```python
import functools
import jax
import jax.numpy as jnp
from jax import lax
from jax.experimental import pallas as pl
from jax.experimental.layout import Layout, with_layout_constraint
from jax.experimental.pallas import tpu as pltpu
from jax.sharding import Mesh, PartitionSpec as P

F32 = jnp.float32
BF16 = jnp.bfloat16
SWAP = [(0, 1), (1, 0)]
META = 16


def dot(a, b, ca, cb):
    return lax.dot_general(a, b, (((ca,), (cb,)), ((), ())), preferred_element_type=F32)


def fused_kernel(
    tok_ref, og_ref, meta_ref, w_ref,
    lay_ref, tg_ref, gg_ref, wg_ref, buf,
    wv, wst, wf, xg, mb, act, acc, po, ps, pr, rx, ggs,
    loc_sem, w_sem, ld_sem,
    xy_s, xy_r, za_s, za_r, zb_s, zb_r, sib_s, sib_r,
    ps_s, ps_r, rx_s, rx_r, gg_s, gg_r, mp_s, mp_r, ml_s, ml_r,
):
    tok, d = tok_ref.shape
    rows = 2 * tok
    hh = wv.shape[1] // 3
    h = hh // 2
    lanes = 128
    per = 3 * hh // lanes
    step = wf.shape[0] // per
    ch = d // 4
    nt = min(256, hh)
    dt = min(512, d)
    me = lax.axis_index("expert")
    z = lax.axis_index("dp")
    core = me % 2
    xx = (me // 2) % 2
    yy = me // 4

    def peer(m, r):
        return (
            ((yy + m // 2) % 2) * 4 + ((xx + m % 2) % 2) * 2 + (core + r) % 2,
            z,
        )

    xn, yn, sib = peer(1, 0), peer(2, 0), peer(0, 1)
    order = [z, 1 + z % 2, (2 + 3 * z) % 5, 3 - 3 * (z // 2)]

    own_half = tok
    cut_a = rows * 11 // 16 // 16 * 16
    a_half = (cut_a // 2 + 8) // 16 * 16
    h1, h2 = (0, own_half), (own_half, rows - own_half)
    a1, a2 = (0, a_half), (a_half, cut_a - a_half)
    whole, pa, pb = (0, rows), (0, cut_a), (cut_a, rows - cut_a)

    def rdma(src, dst, ssem, rsem, dev):
        return pltpu.make_async_remote_copy(
            src_ref=src, dst_ref=dst, send_sem=ssem, recv_sem=rsem,
            device_id=dev, device_id_type=pl.DeviceIdType.MESH,
        )

    def at(r, k, m, part):
        return buf.at[r, k, m, pl.ds(part[0], part[1])]

    def xy(k, i, own):
        p1, p2 = (h1, h2) if own else (a1, a2)
        src, dst, part, dev = [
            (0, 1, p1, xn), (0, 1, p2, xn), (0, 2, p2, yn), (0, 2, p1, yn),
            (1, 3, p1, yn), (2, 3, p2, xn),
        ][i]
        return rdma(at(0, k, src, part), at(0, k, dst, part), xy_s.at[k, i], xy_r.at[k, i], dev)

    def line(k, m, up):
        dev = (me, z + 1) if up else (me, z - 1)
        u = 1 if up else 0
        if m is None:
            return rdma(at(0, k, 0, pa), at(0, k, 0, pa), za_s.at[k, u], za_r.at[k], dev)
        if m == "meta":
            return rdma(mb.at[k], mb.at[k], ml_s.at[k, u], ml_r.at[k], dev)
        return rdma(at(0, k, m, pb), at(0, k, m, pb), zb_s.at[k, m, u], zb_r.at[k, m], dev)

    def on_line(k, m, what):
        @pl.when((k <= z) & (z < 3))
        def _():
            getattr(line(k, m, True), what)()

        @pl.when((k >= z) & (z > 0))
        def _():
            getattr(line(k, m, False), what)()

    def sibling(k, m, i, part):
        return rdma(at(0, k, m, part), at(1, k, m, part), sib_s.at[k, m, i], sib_r.at[k, m, i], sib)

    own = [
        pltpu.make_async_copy(tok_ref, at(0, z, 0, (0, tok)), loc_sem.at[0]),
        pltpu.make_async_copy(og_ref, at(0, z, 0, (tok, tok)), loc_sem.at[1]),
    ]
    for c in own:
        c.start()
    barrier = pltpu.get_barrier_semaphore()
    for i in range(1, 8):
        pl.semaphore_signal(barrier, inc=1, device_id=peer(i // 2, i % 2), device_id_type=pl.DeviceIdType.MESH)

    @pl.when(z > 0)
    def _():
        pl.semaphore_signal(barrier, inc=1, device_id=(me, z - 1), device_id_type=pl.DeviceIdType.MESH)

    @pl.when(z < 3)
    def _():
        pl.semaphore_signal(barrier, inc=1, device_id=(me, z + 1), device_id_type=pl.DeviceIdType.MESH)

    pl.semaphore_wait(barrier, 8 + (z + 1) // 2 % 2)

    mb[z, 0] = meta_ref[...]
    for c in own:
        c.wait()

    def own_first():
        xy(z, 0, True).start()
        xy(z, 2, True).start()
        on_line(z, None, "start")
        for i in range(1, 8):
            near_meta(i).start()

    def own_second():
        xy(z, 1, True).start()
        xy(z, 3, True).start()
        sibling(z, 0, 0, whole).start()

    def own_mid(i):
        xy(z, 2 * i, True).wait_recv()
        xy(z, 4 + i, True).start()

    def own_near(i):
        xy(z, 1 + 2 * i, True).wait_recv()
        sibling(z, 1 + i, 0, whole).start()

    def own_far():
        xy(z, 4, True).wait_recv()
        xy(z, 5, True).wait_recv()
        sibling(z, 3, 0, whole).start()

    def near_meta(i):
        return rdma(meta_ref, mb.at[z, i], mp_s.at[i], mp_r.at[i], peer(i // 2, i % 2))

    def metas():
        for i in range(1, 8):
            near_meta(i).wait_recv()
        on_line(z, "meta", "start")

    def wave(n, m):
        @pl.when(z + n <= 3)
        def _():
            take(z + n, m)

            @pl.when(z > 0)
            def _():
                line(z + n, m, False).start()

        @pl.when(z - n >= 0)
        def _():
            take(z - n, m)

            @pl.when(z < 3)
            def _():
                line(z - n, m, True).start()

    def take(k, m):
        line(k, m, True).wait_recv()
        if m is None:
            sibling(k, 0, 0, pa).start()
        elif m != "meta":
            sibling(k, m, 1, pb).start()

    def far_out(k, i):
        xy(k, i, False).start()
        xy(k, (2, 3)[i], False).start()

    def far_mid(k, i):
        xy(k, 2 * i, False).wait_recv()
        xy(k, 4 + i, False).start()

    def far_near(k, i):
        xy(k, 1 + 2 * i, False).wait_recv()
        sibling(k, 1 + i, 0, pa).start()

    def far_far(k):
        xy(k, 4, False).wait_recv()
        xy(k, 5, False).wait_recv()
        sibling(k, 3, 0, pa).start()

    def raw(c):
        return pltpu.make_async_copy(
            w_ref.at[pl.ds(pl.multiple_of(c * step * per, step * per), step * per)],
            wst.at[c % 2], w_sem.at[c % 2],
        )

    def place(p, j, e):
        return (p * (h // lanes) + j) * 2 + e, p * hh + e * h + j * lanes

    def lay_weights():
        n = d // step
        raw(0).start()

        def chunk(c, carry):
            @pl.when(c + 1 < n)
            def _():
                raw(c + 1).start()

            raw(c).wait()
            wf[...] = wst[c % 2].astype(F32)
            to = pl.ds(pl.multiple_of(c * step, step), step)
            for p in range(3):
                for j in range(h // lanes):
                    for e in range(2):
                        at_row, col = place(p, j, e)
                        wv[to, col : col + lanes] = wf[pl.ds(at_row, step, stride=per), :].astype(BF16)
            return carry

        lax.fori_loop(0, n, chunk, 0)

    def lay_grads():
        for p in range(3):
            for j in range(h // lanes):
                for e in range(2):
                    at_row, col = place(p, j, e)
                    wg_ref[pl.ds(at_row, ch, stride=per), :] = acc[:, col : col + lanes]

    def load(k, s, slot, what):
        for mi in range(2):
            for r in range(2):
                b = mi * 2 + r
                getattr(
                    pltpu.make_async_copy(buf.at[r, k, 2 * s + mi], xg.at[slot, b], ld_sem.at[slot, b]), what
                )()

    def arrived(k, s, mine):
        for m in (2 * s, 2 * s + 1):
            if mine:
                sibling(k, m, 0, whole).wait_recv()
            else:
                sibling(k, m, 0, pa).wait_recv()
                sibling(k, m, 1, pb).wait_recv()

    def first(k, slot, s, mine):
        def tile(n, gg):
            c0 = pl.multiple_of(n * nt, nt)
            xs = xg[slot, :, 0:tok, :].reshape(4 * tok, d)
            gs = xg[slot, :, tok : 2 * tok, :].reshape(4 * tok, d)
            gate = dot(xs, wv[:, pl.ds(c0, nt)], 1, 0)
            up = dot(xs, wv[:, pl.ds(hh + c0, nt)], 1, 0)
            u = dot(gs, wv[:, pl.ds(2 * hh + c0, nt)], 1, 0)
            col = c0 + lax.broadcasted_iota(jnp.int32, (2 * META, nt), 1)
            row = lax.broadcasted_iota(jnp.int32, (2 * META, nt), 0) % META
            sel = (row == 2 * me + (col >= h).astype(jnp.int32)).astype(F32).astype(BF16)
            ps_ = []
            for b in range(4):
                both = jnp.concatenate(
                    [mb[k, 4 * s + b, :, :tok], mb[k, 4 * s + b, :, tok:]], axis=0
                )
                ps_.append(dot(both, sel, 0, 0))
            p = jnp.concatenate(ps_, axis=0)
            s_ = jax.nn.sigmoid(gate)
            act_ = gate * s_
            hidden = act_ * up
            hc = p * u
            act[:, pl.ds(c0, nt)] = (hc * up * (s_ + act_ * (1.0 - s_))).astype(BF16)
            act[:, pl.ds(hh + c0, nt)] = (hc * act_).astype(BF16)
            act[:, pl.ds(2 * hh + c0, nt)] = (p * hidden).astype(BF16)
            if mine:
                uh = u * hidden
                hi = uh.astype(BF16)
                lo = (uh - hi.astype(F32)).astype(BF16)
                own_row = lax.broadcasted_iota(jnp.int32, (8, nt), 0)
                own_col = c0 + lax.broadcasted_iota(jnp.int32, (8, nt), 1)
                pick = (own_row == (own_col >= h).astype(jnp.int32)).astype(F32).astype(BF16)
                gg = gg + dot(pick, hi, 1, 1) + dot(pick, lo, 1, 1)
            return gg

        start = jnp.zeros((8, 4 * tok), F32)
        gg = lax.fori_loop(0, hh // nt, tile, start)
        if mine:
            for b in range(4):
                ggs[4 * s + b] = gg[:, b * tok : (b + 1) * tok]

    def third(slot):
        x0 = pl.multiple_of(z * ch, ch)
        xs = xg[slot, :, 0:tok, pl.ds(x0, ch)].reshape(4 * tok, ch)
        acc[:, 0 : 2 * hh] += dot(xs, act[:, 0 : 2 * hh], 0, 0)
        gs = xg[slot, :, tok : 2 * tok, pl.ds(x0, ch)].reshape(4 * tok, ch)
        acc[:, 2 * hh :] += dot(gs, act[:, 2 * hh :], 0, 0)

    def second(s):
        def tile(n, carry):
            r0 = pl.multiple_of(n * dt, dt)
            out = dot(act[:, 2 * hh :], wv[pl.ds(r0, dt), 2 * hh :], 1, 1).astype(BF16)
            tg = dot(act[:, : 2 * hh], wv[pl.ds(r0, dt), : 2 * hh], 1, 1).astype(BF16)
            for mi in range(2):
                for q, v in ((0, out), (1, tg)):
                    b = 2 * mi * tok
                    po[q, 2 * s + mi, :, pl.ds(r0, dt)] = v[b : b + tok]
                    ps[q, 2 * s + mi, :, pl.ds(r0, dt)] = v[b + tok : b + 2 * tok]
            return carry

        lax.fori_loop(0, d // dt, tile, 0)

    def swap(q, s):
        part = pl.ds(2 * s, 2)
        return rdma(ps.at[q, part], pr.at[q, part], ps_s.at[q, s], ps_r.at[q, s], sib)

    def add(i, j):
        po[i] = (po[i].astype(F32) + j.astype(F32)).astype(BF16)

    def merge(s):
        for q in range(2):
            swap(q, s).wait_recv()
            for m in (2 * s, 2 * s + 1):
                add((q, m), pr[q, m])

    def back(q, i):
        near, far = (1, 2) if q == 0 else (2, 1)
        dev, dev2 = (xn, yn) if q == 0 else (yn, xn)
        if i < 2:
            return rdma(po.at[q, (near, 3)[i]], rx.at[q, i], rx_s.at[q, i], rx_r.at[q, i], dev)
        return rdma(po.at[q, far], rx.at[q, 2], rx_s.at[q, 2], rx_r.at[q, 2], dev2)

    def back_mid(q):
        far = 2 if q == 0 else 1
        back(q, 1).wait_recv()
        add((q, far), rx[q, 1])
        back(q, 2).start()

    def back_end(q, ref):
        back(q, 0).wait_recv()
        back(q, 2).wait_recv()
        ref[...] = (po[q, 0].astype(F32) + rx[q, 0].astype(F32) + rx[q, 2].astype(F32)).astype(BF16)

    def gg_copy(i):
        return rdma(ggs.at[i], gg_ref.at[i], gg_s.at[i], gg_r.at[i], peer(i // 2, i % 2))

    k1, k2, k3 = order[1:]
    own_first()
    acc[...] = jnp.zeros_like(acc)
    lay_weights()
    own_second()
    own_mid(1)
    metas()
    on_line(z, 0, "start")
    own_mid(0)
    wave(1, None)
    own_near(0)
    far_out(k1, 0)
    arrived(z, 0, True)
    load(z, 0, 0, "start")
    own_far()
    far_out(k1, 1)
    on_line(z, 1, "start")
    wave(2, None)
    far_mid(k1, 0)
    own_near(1)
    far_out(k2, 0)
    far_mid(k1, 1)
    load(z, 0, 0, "wait")
    first(z, 0, 0, True)
    wave(1, 1)
    arrived(z, 1, True)
    load(z, 1, 1, "start")
    second(0)
    swap(0, 0).start()
    swap(1, 0).start()
    third(0)
    far_out(k2, 1)
    load(z, 1, 1, "wait")
    first(z, 1, 1, True)
    wave(3, None)
    far_near(k1, 0)
    far_out(k3, 0)
    on_line(z, 2, "start")
    second(1)
    swap(0, 1).start()
    swap(1, 1).start()
    for i in range(1, 8):
        gg_copy(i).start()
    gg_ref[0] = ggs[0]
    far_mid(k2, 1)
    merge(0)
    on_line(z, 3, "start")
    wave(1, 2)
    third(1)
    wave(1, 0)
    wave(1, "meta")
    far_out(k3, 1)
    far_far(k1)
    far_mid(k3, 1)
    far_mid(k2, 0)
    far_mid(k3, 0)
    far_near(k1, 1)
    arrived(k1, 0, False)
    load(k1, 0, 0, "start")
    far_near(k2, 0)
    far_near(k2, 1)
    wave(1, 3)
    load(k1, 0, 0, "wait")
    first(k1, 0, 0, False)
    arrived(k1, 1, False)
    load(k1, 1, 1, "start")
    third(0)
    wave(2, 1)
    wave(2, 0)
    wave(2, "meta")
    merge(1)
    back(0, 1).start()
    back(0, 0).start()
    back(1, 1).start()
    back(1, 0).start()
    far_near(k3, 0)
    far_far(k2)
    load(k1, 1, 1, "wait")
    first(k1, 1, 1, False)
    arrived(k2, 0, False)
    load(k2, 0, 0, "start")
    third(1)
    far_far(k3)
    wave(2, 2)
    load(k2, 0, 0, "wait")
    first(k2, 0, 0, False)
    wave(2, 3)
    third(0)
    arrived(k2, 1, False)
    load(k2, 1, 1, "start")
    wave(3, 0)
    wave(3, "meta")
    wave(3, 1)
    far_near(k3, 1)
    load(k2, 1, 1, "wait")
    first(k2, 1, 1, False)
    back_mid(0)
    arrived(k3, 0, False)
    load(k3, 0, 0, "start")
    third(1)
    back_mid(1)
    wave(3, 3)
    wave(3, 2)
    load(k3, 0, 0, "wait")
    first(k3, 0, 0, False)
    arrived(k3, 1, False)
    load(k3, 1, 1, "start")
    third(0)
    load(k3, 1, 1, "wait")
    first(k3, 1, 1, False)
    third(1)
    lay_grads()
    back_end(1, tg_ref)
    back_end(0, lay_ref)

    for i in range(6):
        xy(z, i, True).wait_send()
    for m in range(4):
        sibling(z, m, 0, whole).wait_send()
    for k in (k1, k2, k3):
        for i in range(6):
            xy(k, i, False).wait_send()
        for m in range(4):
            sibling(k, m, 0, pa).wait_send()
            sibling(k, m, 1, pb).wait_send()
    for k in order:
        on_line(k, None, "wait_send")
        on_line(k, "meta", "wait_send")
        for m in range(4):
            on_line(k, m, "wait_send")
    for q in range(2):
        for s in range(2):
            swap(q, s).wait_send()
        for i in range(3):
            back(q, i).wait_send()
    for i in range(1, 8):
        gg_copy(i).wait_recv()
        gg_copy(i).wait_send()
        near_meta(i).wait_send()


def fused(tokens, expert_ids, gate_probs, expert_weights, out_grad):
    tok, top = expert_ids.shape
    d = tokens.shape[1]
    local_experts, h = expert_weights.shape[2:]
    hh = local_experts * h
    experts = 8 * local_experts
    rows = 2 * tok
    me = lax.axis_index("expert")

    hot = expert_ids[:, :, None] == jnp.arange(experts)
    p = jnp.sum(jnp.where(hot, gate_probs[:, :, None], 0.0), axis=1).T
    hi = lax.reduce_precision(p, 8, 7)
    meta = jnp.concatenate([hi, p - hi], axis=1).astype(BF16)
    lanes = 128
    w = with_layout_constraint(
        expert_weights.reshape(d, 3, local_experts, h // lanes, lanes),
        Layout(major_to_minor=(0, 1, 3, 2, 4)),
    )
    per = 3 * hh // lanes
    w = jnp.transpose(w, (0, 1, 3, 2, 4)).reshape(d * per, lanes)
    step = 128

    any_ = pl.BlockSpec(memory_space=pl.ANY)
    vmem = pl.BlockSpec(memory_space=pltpu.VMEM)
    dma = pltpu.SemaphoreType.DMA
    lay, tg, gg, wg, _ = pl.pallas_call(
        fused_kernel,
        out_shape=[
            jax.ShapeDtypeStruct((tok, d), BF16),
            jax.ShapeDtypeStruct((tok, d), BF16),
            jax.ShapeDtypeStruct((8, 8, tok), F32),
            jax.ShapeDtypeStruct((d // 4 * per, lanes), F32),
            jax.ShapeDtypeStruct((2, 4, 4, rows, d), BF16),
        ],
        in_specs=[any_, any_, vmem, any_],
        out_specs=[vmem, vmem, vmem, vmem, any_],
        scratch_shapes=[
            pltpu.VMEM((d, 3 * hh), BF16),
            pltpu.VMEM((2, step * per, lanes), BF16),
            pltpu.VMEM((step * per, lanes), F32),
            pltpu.VMEM((2, 4, rows, d), BF16),
            pltpu.VMEM((4, 8, META, 2 * tok), BF16),
            pltpu.VMEM((4 * tok, 3 * hh), BF16),
            pltpu.VMEM((d // 4, 3 * hh), F32),
            pltpu.VMEM((2, 4, tok, d), BF16),
            pltpu.VMEM((2, 4, tok, d), BF16),
            pltpu.VMEM((2, 4, tok, d), BF16),
            pltpu.VMEM((2, 3, tok, d), BF16),
            pltpu.VMEM((8, 8, tok), F32),
            dma((2,)), dma((2,)), dma((2, 4)),
            dma((4, 6)), dma((4, 6)), dma((4, 2)), dma((4,)),
            dma((4, 4, 2)), dma((4, 4)), dma((4, 4, 2)), dma((4, 4, 2)),
            dma((2, 2)), dma((2, 2)), dma((2, 3)), dma((2, 3)), dma((8,)), dma((8,)),
            dma((8,)), dma((8,)), dma((4, 2)), dma((4,)),
        ],
        compiler_params=pltpu.CompilerParams(
            collective_id=0, has_side_effects=True, vmem_limit_bytes=60 * 1024 * 1024
        ),
    )(tokens, out_grad, meta, w)

    rel = jnp.arange(8)
    source = (
        (me // 4 + rel // 4) % 2 * 4 + (me // 2 + rel // 2) % 2 * 2 + (me + rel) % 2
    )
    named = source[:, None] * local_experts + jnp.arange(local_experts)
    match = expert_ids[:, :, None, None] == named
    value = jnp.transpose(gg[:, :local_experts], (2, 0, 1))[:, None]
    gate_grad = jnp.sum(jnp.where(match, value, 0.0), axis=(2, 3))
    wg = jnp.transpose(wg.reshape(d // 4, 3, h // lanes, local_experts, lanes), (0, 1, 3, 2, 4))
    wg = with_layout_constraint(wg, Layout(major_to_minor=(0, 1, 3, 2, 4)))
    return lay, tg, gate_grad, wg.reshape(d // 4, 3, local_experts, h)


def gather(rows):
    n = lax.axis_size("chip")
    own = [rows] + [
        lax.ppermute(rows, "chip", [(i, i ^ k) for i in range(n)]) for k in range(1, n)
    ]
    own = jnp.concatenate(own, axis=0)
    return jnp.concatenate([own, lax.ppermute(own, "core", SWAP)], axis=0)


def scatter(own, other):
    n = lax.axis_size("chip")
    me = lax.axis_index("chip")
    total = own + lax.ppermute(other, "core", SWAP).astype(F32)
    total = total.astype(other.dtype).reshape((n, -1) + own.shape[1:])
    total = jnp.concatenate(
        [lax.dynamic_index_in_dim(total, me ^ k, 0, keepdims=False) for k in range(n)],
        axis=0,
    )
    return lax.psum_scatter(total, "chip", scatter_dimension=0, tiled=True)


def line_scatter(grad):
    n = lax.axis_size("dp")
    me = lax.axis_index("dp")
    rows = grad.shape[0] // n

    def chunk(i):
        i = jnp.clip(i, 0, n - 1)
        return lax.dynamic_slice_in_dim(grad, i * rows, rows, 0).astype(F32)

    up = down = None
    for t in range(n - 1):
        a = chunk(n - 1 - t + me)
        b = chunk(t - (n - 1) + me)
        if t:
            a = a + up.astype(F32)
            b = b + down.astype(F32)
        up = lax.ppermute(a.astype(BF16), "dp", [(i, i + 1) for i in range(t + 1)])
        down = lax.ppermute(
            b.astype(BF16), "dp", [(i, i - 1) for i in range(n - 1 - t, n)]
        )
    return chunk(me) + up.astype(F32) + down.astype(F32)


def local(tokens, expert_ids, gate_probs, expert_weights, out_grad):
    tok_count, top_count = expert_ids.shape
    d = tokens.shape[1]
    chips = lax.axis_size("chip")
    me = lax.axis_index("chip") * 2 + lax.axis_index("core")
    local_experts, h = expert_weights.shape[2:]
    half = chips * tok_count
    eh = local_experts * h

    x = gather(tokens)
    small = gather(jnp.concatenate([expert_ids.astype(F32), gate_probs], axis=1))
    g = gather(out_grad)
    ids = small[:, :top_count].astype(jnp.int32)
    probs = small[:, top_count:]

    hits = [ids == me * local_experts + i for i in range(local_experts)]
    p = jnp.concatenate(
        [
            jnp.broadcast_to(
                jnp.sum(jnp.where(hit, probs, 0.0), axis=1, keepdims=True), (2 * half, h)
            )
            for hit in hits
        ],
        axis=1,
    )

    w = expert_weights.reshape(d, 3 * eh)
    wgu = w[:, : 2 * eh]
    wd = w[:, 2 * eh :]

    a = dot(x, wgu, 1, 0)
    gate = a[:, :eh]
    up = a[:, eh:]
    s = jax.nn.sigmoid(gate)
    hidden = gate * s * up
    ph = (p * hidden).astype(BF16)
    down_grad = line_scatter(dot(g, ph, 0, 0).astype(BF16))

    u = dot(g, wd, 1, 0)
    hc = p * u
    gc = (hc * up * s * (1.0 + gate * (1.0 - s))).astype(BF16)
    uc = (hc * gate * s).astype(BF16)
    gate_part = line_scatter(dot(x, gc, 0, 0).astype(BF16))
    up_part = line_scatter(dot(x, uc, 0, 0).astype(BF16))

    other = dot(ph[half:], wd, 1, 1).astype(BF16)
    layer_out = scatter(dot(ph[:half], wd, 1, 1), other)

    cots = jnp.concatenate([gc, uc], axis=1)
    other = dot(cots[half:], wgu, 1, 1).astype(BF16)
    token_grad = scatter(dot(cots[:half], wgu, 1, 1), other)

    uh = u * hidden
    ggk = sum(
        jnp.where(hit, jnp.sum(uh[:, i * h : (i + 1) * h], axis=1, keepdims=True), 0.0)
        for i, hit in enumerate(hits)
    )
    gate_grad = scatter(ggk[:half], ggk[half:])

    weight_grad = jnp.stack([gate_part, up_part, down_grad], axis=1)
    weight_grad = weight_grad.reshape(-1, 3, local_experts, h)
    return (layer_out, token_grad, gate_grad, weight_grad)


def solution(mesh):
    experts, groups = mesh.devices.shape
    if (experts, groups) == (8, 4):
        tok = P(("expert", "dp"), None)
        return jax.shard_map(
            fused,
            mesh=mesh,
            in_specs=(tok, tok, tok, P(None, None, "expert", None), tok),
            out_specs=(tok, tok, tok, P("dp", None, "expert", None)),
            check_vma=False,
        )
    split = Mesh(
        mesh.devices.reshape(experts // 2, 2, groups), ("chip", "core", "dp")
    )
    tok = P(("chip", "core", "dp"), None)
    wsp = P(None, None, ("chip", "core"), None)
    return jax.shard_map(
        local,
        mesh=split,
        in_specs=(tok, tok, tok, wsp, tok),
        out_specs=(tok, tok, tok, P("dp", None, ("chip", "core"), None)),
        check_vma=False,
    )
```

```python
import functools
import jax
import jax.numpy as jnp
from jax import lax
from jax.experimental import pallas as pl
from jax.experimental.layout import Layout, with_layout_constraint
from jax.experimental.pallas import tpu as pltpu
from jax.sharding import Mesh, PartitionSpec as P

F32 = jnp.float32
BF16 = jnp.bfloat16
SWAP = [(0, 1), (1, 0)]
META = 16
LANES = 128


def dot(a, b, ca, cb):
    return lax.dot_general(a, b, (((ca,), (cb,)), ((), ())), preferred_element_type=F32)


def place(h, p, j, e):
    return (p * (h // LANES) + j) * 2 + e, (2 * p + e) * h + j * LANES


def fused_kernel(
    tok_ref, og_ref, meta_ref, w_ref,
    lay_ref, tg_ref, gg_ref, acc, buf,
    wv, wst, wf, xg, mb, gu, act, po, ps, pr, rx, ggs,
    loc_sem, w_sem, ld_sem,
    xy_s, xy_r, za_s, za_r, zb_s, zb_r, sib_s, sib_r,
    ps_s, ps_r, rx_s, rx_r, gg_s, gg_r, mp_s, mp_r, ml_s, ml_r,
):
    tok, d = tok_ref.shape
    rows = 2 * tok
    hh = wv.shape[1] // 3
    h = hh // 2
    per = 3 * hh // LANES
    step = wf.shape[0] // per
    ch = d // 4
    nt = min(256, hh)
    dt = min(512, d)
    me = lax.axis_index("expert")
    z = lax.axis_index("dp")
    core = me % 2
    xx = (me // 2) % 2
    yy = me // 4

    def peer(m, r):
        return (
            ((yy + m // 2) % 2) * 4 + ((xx + m % 2) % 2) * 2 + (core + r) % 2,
            z,
        )

    xn, yn, sib = peer(1, 0), peer(2, 0), peer(0, 1)
    order = [z, 1 + z % 2, (2 + 3 * z) % 5, 3 - 3 * (z // 2)]

    own_half = tok
    cut_a = rows * 11 // 16 // 16 * 16
    a_half = (cut_a // 2 + 8) // 16 * 16
    h1, h2 = (0, own_half), (own_half, rows - own_half)
    a1, a2 = (0, a_half), (a_half, cut_a - a_half)
    whole, pa, pb = (0, rows), (0, cut_a), (cut_a, rows - cut_a)

    def rdma(src, dst, ssem, rsem, dev):
        return pltpu.make_async_remote_copy(
            src_ref=src, dst_ref=dst, send_sem=ssem, recv_sem=rsem,
            device_id=dev, device_id_type=pl.DeviceIdType.MESH,
        )

    def at(r, k, m, part):
        return buf.at[r, k, m, pl.ds(part[0], part[1])]

    def xy(k, i, own):
        p1, p2 = (h1, h2) if own else (a1, a2)
        src, dst, part, dev = [
            (0, 1, p1, xn), (0, 1, p2, xn), (0, 2, p2, yn), (0, 2, p1, yn),
            (1, 3, p1, yn), (2, 3, p2, xn),
        ][i]
        return rdma(at(0, k, src, part), at(0, k, dst, part), xy_s.at[k, i], xy_r.at[k, i], dev)

    def line(k, m, up):
        dev = (me, z + 1) if up else (me, z - 1)
        u = 1 if up else 0
        if m is None:
            return rdma(at(0, k, 0, pa), at(0, k, 0, pa), za_s.at[k, u], za_r.at[k], dev)
        if m == "meta":
            return rdma(mb.at[k], mb.at[k], ml_s.at[k, u], ml_r.at[k], dev)
        return rdma(at(0, k, m, pb), at(0, k, m, pb), zb_s.at[k, m, u], zb_r.at[k, m], dev)

    def on_line(k, m, what):
        @pl.when((k <= z) & (z < 3))
        def _():
            getattr(line(k, m, True), what)()

        @pl.when((k >= z) & (z > 0))
        def _():
            getattr(line(k, m, False), what)()

    def sibling(k, m, i, part):
        return rdma(at(0, k, m, part), at(1, k, m, part), sib_s.at[k, m, i], sib_r.at[k, m, i], sib)

    own = [
        pltpu.make_async_copy(tok_ref, xg.at[0, 0, pl.ds(0, tok)], loc_sem.at[0]),
        pltpu.make_async_copy(og_ref, xg.at[0, 0, pl.ds(tok, tok)], loc_sem.at[1]),
    ]
    held = pltpu.make_async_copy(xg.at[0, 0], buf.at[0, z, 0], loc_sem.at[2])
    for c in own:
        c.start()
    barrier = pltpu.get_barrier_semaphore()
    for i in range(1, 8):
        pl.semaphore_signal(barrier, inc=1, device_id=peer(i // 2, i % 2), device_id_type=pl.DeviceIdType.MESH)

    @pl.when(z > 0)
    def _():
        pl.semaphore_signal(barrier, inc=1, device_id=(me, z - 1), device_id_type=pl.DeviceIdType.MESH)

    @pl.when(z < 3)
    def _():
        pl.semaphore_signal(barrier, inc=1, device_id=(me, z + 1), device_id_type=pl.DeviceIdType.MESH)

    mb[z, 0] = meta_ref[...]
    for c in own:
        c.wait()
    held.start()
    pl.semaphore_wait(barrier, 8 + (z + 1) // 2 % 2)
    held.wait()

    def own_first():
        xy(z, 0, True).start()
        xy(z, 2, True).start()
        on_line(z, None, "start")
        for i in range(1, 8):
            near_meta(i).start()

    def own_second():
        xy(z, 1, True).start()
        xy(z, 3, True).start()
        sibling(z, 0, 0, whole).start()

    def own_mid(i):
        xy(z, 2 * i, True).wait_recv()
        xy(z, 4 + i, True).start()

    def own_near(i):
        xy(z, 1 + 2 * i, True).wait_recv()
        sibling(z, 1 + i, 0, whole).start()

    def own_far():
        xy(z, 4, True).wait_recv()
        xy(z, 5, True).wait_recv()
        sibling(z, 3, 0, whole).start()

    def near_meta(i):
        return rdma(meta_ref, mb.at[z, i], mp_s.at[i], mp_r.at[i], peer(i // 2, i % 2))

    def metas():
        for i in range(1, 8):
            near_meta(i).wait_recv()
        on_line(z, "meta", "start")

    def wave(n, m):
        @pl.when(z + n <= 3)
        def _():
            take(z + n, m)

            @pl.when(z > 0)
            def _():
                line(z + n, m, False).start()

        @pl.when(z - n >= 0)
        def _():
            take(z - n, m)

            @pl.when(z < 3)
            def _():
                line(z - n, m, True).start()

    def take(k, m):
        line(k, m, True).wait_recv()
        if m is None:
            sibling(k, 0, 0, pa).start()
        elif m != "meta":
            sibling(k, m, 1, pb).start()

    def far_out(k, i):
        xy(k, i, False).start()
        xy(k, (2, 3)[i], False).start()

    def far_mid(k, i):
        xy(k, 2 * i, False).wait_recv()
        xy(k, 4 + i, False).start()

    def far_near(k, i):
        xy(k, 1 + 2 * i, False).wait_recv()
        sibling(k, 1 + i, 0, pa).start()

    def far_far(k):
        xy(k, 4, False).wait_recv()
        xy(k, 5, False).wait_recv()
        sibling(k, 3, 0, pa).start()

    def raw(c):
        return pltpu.make_async_copy(
            w_ref.at[pl.ds(pl.multiple_of(c * step * per, step * per), step * per)],
            wst.at[c % 2], w_sem.at[c % 2],
        )

    def lay_weights():
        n = d // step
        raw(0).start()

        def chunk(c, carry):
            @pl.when(c + 1 < n)
            def _():
                raw(c + 1).start()

            raw(c).wait()
            wf[...] = wst[c % 2].astype(F32)
            to = pl.ds(pl.multiple_of(c * step, step), step)
            for p in range(3):
                for j in range(h // LANES):
                    for e in range(2):
                        at_row, col = place(h, p, j, e)
                        wv[to, col : col + LANES] = wf[pl.ds(at_row, step, stride=per), :].astype(BF16)
            return carry

        lax.fori_loop(0, n, chunk, 0)

    def load(k, s, i, what):
        for b in range(4):
            part = pl.ds(i * tok, tok)
            c = pltpu.make_async_copy(
                buf.at[b % 2, k, 2 * s + b // 2, part], xg.at[s, b, part], ld_sem.at[s, b, i]
            )
            getattr(c, what)()

    def load_x(k, s, mine):
        for m in (2 * s, 2 * s + 1):
            sibling(k, m, 0, whole if mine else pa).wait_recv()
        load(k, s, 0, "start")

    def load_g(k, s, mine):
        if not mine:
            for m in (2 * s, 2 * s + 1):
                sibling(k, m, 1, pb).wait_recv()
        load(k, s, 1, "start")

    def gates(k, s):
        load(k, s, 0, "wait")

        def tile(n, carry):
            c0 = pl.multiple_of(n * nt, nt)
            xs = xg[s, :, 0:tok, :].reshape(4 * tok, d)
            for i in range(2):
                gu[s, i, :, pl.ds(c0, nt)] = dot(xs, wv[:, pl.ds(i * hh + c0, nt)], 1, 0)
            return carry

        lax.fori_loop(0, hh // nt, tile, 0)

    def hidden_cots(k, s, mine):
        load(k, s, 1, "wait")

        def tile(n, gg):
            c0 = pl.multiple_of(n * nt, nt)
            gs = xg[s, :, tok:, :].reshape(4 * tok, d)
            u = dot(gs, wv[:, pl.ds(2 * hh + c0, nt)], 1, 0)
            gate = gu[s, 0, :, pl.ds(c0, nt)]
            up = gu[s, 1, :, pl.ds(c0, nt)]
            col = c0 + lax.broadcasted_iota(jnp.int32, (2 * META, nt), 1)
            row = lax.broadcasted_iota(jnp.int32, (2 * META, nt), 0) % META
            sel = (row == 2 * me + (col >= h).astype(jnp.int32)).astype(F32).astype(BF16)
            shares = []
            for b in range(4):
                both = jnp.concatenate(
                    [mb[k, 4 * s + b, :, :tok], mb[k, 4 * s + b, :, tok:]], axis=0
                )
                shares.append(dot(both, sel, 0, 0))
            p = jnp.concatenate(shares, axis=0)
            sig = jax.nn.sigmoid(gate)
            silu = gate * sig
            hidden = silu * up
            hc = p * u
            act[:, pl.ds(c0, nt)] = (hc * up * (sig + silu * (1.0 - sig))).astype(BF16)
            act[:, pl.ds(hh + c0, nt)] = (hc * silu).astype(BF16)
            act[:, pl.ds(2 * hh + c0, nt)] = (p * hidden).astype(BF16)
            if mine:
                uh = u * hidden
                hi = uh.astype(BF16)
                lo = (uh - hi.astype(F32)).astype(BF16)
                own_row = lax.broadcasted_iota(jnp.int32, (8, nt), 0)
                own_col = c0 + lax.broadcasted_iota(jnp.int32, (8, nt), 1)
                pick = (own_row == (own_col >= h).astype(jnp.int32)).astype(F32).astype(BF16)
                gg = gg + dot(pick, hi, 1, 1) + dot(pick, lo, 1, 1)
            return gg

        start = jnp.zeros((8, 4 * tok), F32)
        gg = lax.fori_loop(0, hh // nt, tile, start)
        if mine:
            for b in range(4):
                ggs[4 * s + b] = gg[:, b * tok : (b + 1) * tok]

    def third(s):
        x0 = pl.multiple_of(z * ch, ch)
        xs = xg[s, :, 0:tok, pl.ds(x0, ch)].reshape(4 * tok, ch)
        acc[:, 0 : 2 * hh] += dot(xs, act[:, 0 : 2 * hh], 0, 0)
        gs = xg[s, :, tok:, pl.ds(x0, ch)].reshape(4 * tok, ch)
        acc[:, 2 * hh :] += dot(gs, act[:, 2 * hh :], 0, 0)

    def second(s):
        def tile(n, carry):
            r0 = pl.multiple_of(n * dt, dt)
            out = dot(act[:, 2 * hh :], wv[pl.ds(r0, dt), 2 * hh :], 1, 1).astype(BF16)
            tg = dot(act[:, : 2 * hh], wv[pl.ds(r0, dt), : 2 * hh], 1, 1).astype(BF16)
            for mi in range(2):
                for q, v in ((0, out), (1, tg)):
                    b = 2 * mi * tok
                    po[q, 2 * s + mi, :, pl.ds(r0, dt)] = v[b : b + tok]
                    ps[q, 2 * s + mi, :, pl.ds(r0, dt)] = v[b + tok : b + 2 * tok]
            return carry

        lax.fori_loop(0, d // dt, tile, 0)

    def swap(q, s):
        part = pl.ds(2 * s, 2)
        return rdma(ps.at[q, part], pr.at[q, part], ps_s.at[q, s], ps_r.at[q, s], sib)

    def add(i, j):
        po[i] = (po[i].astype(F32) + j.astype(F32)).astype(BF16)

    def merge(s):
        for q in range(2):
            swap(q, s).wait_recv()
            for m in (2 * s, 2 * s + 1):
                add((q, m), pr[q, m])

    def back(q, i):
        near, far = (1, 2) if q == 0 else (2, 1)
        dev, dev2 = (xn, yn) if q == 0 else (yn, xn)
        if i < 2:
            return rdma(po.at[q, (near, 3)[i]], rx.at[q, i], rx_s.at[q, i], rx_r.at[q, i], dev)
        return rdma(po.at[q, far], rx.at[q, 2], rx_s.at[q, 2], rx_r.at[q, 2], dev2)

    def back_mid(q):
        far = 2 if q == 0 else 1
        back(q, 1).wait_recv()
        add((q, far), rx[q, 1])
        back(q, 2).start()

    def back_end(q, ref):
        back(q, 0).wait_recv()
        back(q, 2).wait_recv()
        ref[...] = (po[q, 0].astype(F32) + rx[q, 0].astype(F32) + rx[q, 2].astype(F32)).astype(BF16)

    def gg_copy(i):
        return rdma(ggs.at[i], gg_ref.at[i], gg_s.at[i], gg_r.at[i], peer(i // 2, i % 2))

    k1, k2, k3 = order[1:]
    own_first()
    acc[...] = jnp.zeros_like(acc)
    lay_weights()
    own_second()
    own_mid(0)
    metas()
    on_line(z, 0, "start")
    wave(1, None)
    own_mid(1)
    far_out(k1, 0)
    own_near(0)
    load_x(z, 0, True)
    far_out(k1, 1)
    on_line(z, 1, "start")
    wave(2, None)
    far_mid(k1, 1)
    far_out(k2, 0)
    own_near(1)
    far_mid(k1, 0)
    load_g(z, 0, True)
    own_far()
    gates(z, 0)
    far_near(k1, 1)
    on_line(z, 2, "start")
    far_out(k2, 1)
    wave(3, None)
    hidden_cots(z, 0, True)
    far_near(k1, 0)
    wave(1, 1)
    far_out(k3, 0)
    second(0)
    swap(0, 0).start()
    swap(1, 0).start()
    load_x(z, 1, True)
    far_mid(k2, 0)
    third(0)
    load_g(z, 1, True)
    on_line(z, 3, "start")
    far_mid(k2, 1)
    gates(z, 1)
    load_x(k1, 0, False)
    hidden_cots(z, 1, True)
    wave(1, 0)
    wave(1, "meta")
    far_far(k1)
    wave(1, 2)
    second(1)
    swap(0, 1).start()
    swap(1, 1).start()
    for i in range(1, 8):
        gg_copy(i).start()
    gg_ref[0] = ggs[0]
    load_g(k1, 0, False)
    far_mid(k3, 1)
    third(1)
    far_out(k3, 1)
    gates(k1, 0)
    load_x(k1, 1, False)
    merge(0)
    merge(1)
    wave(1, 3)
    far_mid(k3, 0)
    far_near(k2, 0)
    far_near(k2, 1)
    hidden_cots(k1, 0, False)
    third(0)
    gates(k1, 1)
    wave(2, 1)
    far_far(k2)
    back(1, 1).start()
    back(1, 0).start()
    load_x(k2, 0, False)
    wave(2, 0)
    wave(2, "meta")
    load_g(k1, 1, False)
    back(0, 1).start()
    back(0, 0).start()
    load_g(k2, 0, False)
    hidden_cots(k1, 1, False)
    far_near(k3, 0)
    third(1)
    gates(k2, 0)
    wave(2, 2)
    load_x(k2, 1, False)
    hidden_cots(k2, 0, False)
    third(0)
    load_x(k3, 0, False)
    far_far(k3)
    gates(k2, 1)
    wave(2, 3)
    far_near(k3, 1)
    gates(k3, 0)
    wave(3, 0)
    wave(3, "meta")
    load_g(k2, 1, False)
    wave(3, 1)
    hidden_cots(k2, 1, False)
    back_mid(1)
    load_g(k3, 0, False)
    back_mid(0)
    third(1)
    wave(3, 2)
    load_x(k3, 1, False)
    hidden_cots(k3, 0, False)
    wave(3, 3)
    gates(k3, 1)
    load_g(k3, 1, False)
    third(0)
    hidden_cots(k3, 1, False)
    third(1)
    back_end(1, tg_ref)
    back_end(0, lay_ref)

    for i in range(6):
        xy(z, i, True).wait_send()
    for m in range(4):
        sibling(z, m, 0, whole).wait_send()
    for k in (k1, k2, k3):
        for i in range(6):
            xy(k, i, False).wait_send()
        for m in range(4):
            sibling(k, m, 0, pa).wait_send()
            sibling(k, m, 1, pb).wait_send()
    for k in order:
        on_line(k, None, "wait_send")
        on_line(k, "meta", "wait_send")
        for m in range(4):
            on_line(k, m, "wait_send")
    for q in range(2):
        for s in range(2):
            swap(q, s).wait_send()
        for i in range(3):
            back(q, i).wait_send()
    for i in range(1, 8):
        gg_copy(i).wait_recv()
        gg_copy(i).wait_send()
        near_meta(i).wait_send()


def finish_kernel(acc_ref, lay_ref, tg_ref, wg_out, lay_out, tg_out):
    rows, cols = acc_ref.shape
    h = cols // 6
    for p in range(3):
        for j in range(h // LANES):
            for e in range(2):
                at_row, col = place(h, p, j, e)
                wg_out[pl.ds(at_row, rows, stride=cols // LANES), :] = acc_ref[:, col : col + LANES]
    lay_out[...] = lay_ref[...]
    tg_out[...] = tg_ref[...]


def finish(acc, lay, tg):
    rows, cols = acc.shape
    n = 4
    per = cols // LANES
    tall = pl.BlockSpec((rows // n, cols), lambda i: (i, 0))
    wide = pl.BlockSpec((lay.shape[0] // n, lay.shape[1]), lambda i: (i, 0))
    return pl.pallas_call(
        finish_kernel,
        grid=(n,),
        out_shape=[
            jax.ShapeDtypeStruct((rows * per, LANES), F32),
            jax.ShapeDtypeStruct(lay.shape, lay.dtype),
            jax.ShapeDtypeStruct(tg.shape, tg.dtype),
        ],
        in_specs=[tall, wide, wide],
        out_specs=[pl.BlockSpec((rows // n * per, LANES), lambda i: (i, 0)), wide, wide],
        compiler_params=pltpu.CompilerParams(vmem_limit_bytes=60 * 1024 * 1024),
    )(acc, lay, tg)


def fused(tokens, expert_ids, gate_probs, expert_weights, out_grad):
    tok, top = expert_ids.shape
    d = tokens.shape[1]
    local_experts, h = expert_weights.shape[2:]
    hh = local_experts * h
    experts = 8 * local_experts
    rows = 2 * tok
    me = lax.axis_index("expert")

    hot = expert_ids[:, :, None] == jnp.arange(experts)
    p = jnp.sum(jnp.where(hot, gate_probs[:, :, None], 0.0), axis=1).T
    hi = lax.reduce_precision(p, 8, 7)
    meta = jnp.concatenate([hi, p - hi], axis=1).astype(BF16)
    w = with_layout_constraint(
        expert_weights.reshape(d, 3, local_experts, h // LANES, LANES),
        Layout(major_to_minor=(0, 1, 3, 2, 4)),
    )
    per = 3 * hh // LANES
    w = jnp.transpose(w, (0, 1, 3, 2, 4)).reshape(d * per, LANES)
    step = 128

    any_ = pl.BlockSpec(memory_space=pl.ANY)
    vmem = pl.BlockSpec(memory_space=pltpu.VMEM)
    dma = pltpu.SemaphoreType.DMA
    lay, tg, gg, acc, _ = pl.pallas_call(
        fused_kernel,
        out_shape=[
            jax.ShapeDtypeStruct((tok, d), BF16),
            jax.ShapeDtypeStruct((tok, d), BF16),
            jax.ShapeDtypeStruct((8, 8, tok), F32),
            jax.ShapeDtypeStruct((d // 4, 3 * hh), F32),
            jax.ShapeDtypeStruct((2, 4, 4, rows, d), BF16),
        ],
        in_specs=[any_, any_, vmem, any_],
        out_specs=[vmem, vmem, vmem, vmem, any_],
        scratch_shapes=[
            pltpu.VMEM((d, 3 * hh), BF16),
            pltpu.VMEM((2, step * per, LANES), BF16),
            pltpu.VMEM((step * per, LANES), F32),
            pltpu.VMEM((2, 4, rows, d), BF16),
            pltpu.VMEM((4, 8, META, 2 * tok), BF16),
            pltpu.VMEM((2, 2, 4 * tok, hh), F32),
            pltpu.VMEM((4 * tok, 3 * hh), BF16),
            pltpu.VMEM((2, 4, tok, d), BF16),
            pltpu.VMEM((2, 4, tok, d), BF16),
            pltpu.VMEM((2, 4, tok, d), BF16),
            pltpu.VMEM((2, 3, tok, d), BF16),
            pltpu.VMEM((8, 8, tok), F32),
            dma((3,)), dma((2,)), dma((2, 4, 2)),
            dma((4, 6)), dma((4, 6)), dma((4, 2)), dma((4,)),
            dma((4, 4, 2)), dma((4, 4)), dma((4, 4, 2)), dma((4, 4, 2)),
            dma((2, 2)), dma((2, 2)), dma((2, 3)), dma((2, 3)), dma((8,)), dma((8,)),
            dma((8,)), dma((8,)), dma((4, 2)), dma((4,)),
        ],
        compiler_params=pltpu.CompilerParams(
            collective_id=0, has_side_effects=True, vmem_limit_bytes=60 * 1024 * 1024
        ),
    )(tokens, out_grad, meta, w)

    wg, lay, tg = finish(acc, lay, tg)

    rel = jnp.arange(8)
    source = (
        (me // 4 + rel // 4) % 2 * 4 + (me // 2 + rel // 2) % 2 * 2 + (me + rel) % 2
    )
    named = source[:, None] * local_experts + jnp.arange(local_experts)
    match = expert_ids[:, :, None, None] == named
    value = jnp.transpose(gg[:, :local_experts], (2, 0, 1))[:, None]
    gate_grad = jnp.sum(jnp.where(match, value, 0.0), axis=(2, 3))
    wg = jnp.transpose(wg.reshape(d // 4, 3, h // LANES, local_experts, LANES), (0, 1, 3, 2, 4))
    wg = with_layout_constraint(wg, Layout(major_to_minor=(0, 1, 3, 2, 4)))
    return lay, tg, gate_grad, wg.reshape(d // 4, 3, local_experts, h)


def gather(rows):
    n = lax.axis_size("chip")
    own = [rows] + [
        lax.ppermute(rows, "chip", [(i, i ^ k) for i in range(n)]) for k in range(1, n)
    ]
    own = jnp.concatenate(own, axis=0)
    return jnp.concatenate([own, lax.ppermute(own, "core", SWAP)], axis=0)


def scatter(own, other):
    n = lax.axis_size("chip")
    me = lax.axis_index("chip")
    total = own + lax.ppermute(other, "core", SWAP).astype(F32)
    total = total.astype(other.dtype).reshape((n, -1) + own.shape[1:])
    total = jnp.concatenate(
        [lax.dynamic_index_in_dim(total, me ^ k, 0, keepdims=False) for k in range(n)],
        axis=0,
    )
    return lax.psum_scatter(total, "chip", scatter_dimension=0, tiled=True)


def line_scatter(grad):
    n = lax.axis_size("dp")
    me = lax.axis_index("dp")
    rows = grad.shape[0] // n

    def chunk(i):
        i = jnp.clip(i, 0, n - 1)
        return lax.dynamic_slice_in_dim(grad, i * rows, rows, 0).astype(F32)

    up = down = None
    for t in range(n - 1):
        a = chunk(n - 1 - t + me)
        b = chunk(t - (n - 1) + me)
        if t:
            a = a + up.astype(F32)
            b = b + down.astype(F32)
        up = lax.ppermute(a.astype(BF16), "dp", [(i, i + 1) for i in range(t + 1)])
        down = lax.ppermute(
            b.astype(BF16), "dp", [(i, i - 1) for i in range(n - 1 - t, n)]
        )
    return chunk(me) + up.astype(F32) + down.astype(F32)


def local(tokens, expert_ids, gate_probs, expert_weights, out_grad):
    tok_count, top_count = expert_ids.shape
    d = tokens.shape[1]
    chips = lax.axis_size("chip")
    me = lax.axis_index("chip") * 2 + lax.axis_index("core")
    local_experts, h = expert_weights.shape[2:]
    half = chips * tok_count
    eh = local_experts * h

    x = gather(tokens)
    small = gather(jnp.concatenate([expert_ids.astype(F32), gate_probs], axis=1))
    g = gather(out_grad)
    ids = small[:, :top_count].astype(jnp.int32)
    probs = small[:, top_count:]

    hits = [ids == me * local_experts + i for i in range(local_experts)]
    p = jnp.concatenate(
        [
            jnp.broadcast_to(
                jnp.sum(jnp.where(hit, probs, 0.0), axis=1, keepdims=True), (2 * half, h)
            )
            for hit in hits
        ],
        axis=1,
    )

    w = expert_weights.reshape(d, 3 * eh)
    wgu = w[:, : 2 * eh]
    wd = w[:, 2 * eh :]

    a = dot(x, wgu, 1, 0)
    gate = a[:, :eh]
    up = a[:, eh:]
    s = jax.nn.sigmoid(gate)
    hidden = gate * s * up
    ph = (p * hidden).astype(BF16)
    down_grad = line_scatter(dot(g, ph, 0, 0).astype(BF16))

    u = dot(g, wd, 1, 0)
    hc = p * u
    gc = (hc * up * s * (1.0 + gate * (1.0 - s))).astype(BF16)
    uc = (hc * gate * s).astype(BF16)
    gate_part = line_scatter(dot(x, gc, 0, 0).astype(BF16))
    up_part = line_scatter(dot(x, uc, 0, 0).astype(BF16))

    other = dot(ph[half:], wd, 1, 1).astype(BF16)
    layer_out = scatter(dot(ph[:half], wd, 1, 1), other)

    cots = jnp.concatenate([gc, uc], axis=1)
    other = dot(cots[half:], wgu, 1, 1).astype(BF16)
    token_grad = scatter(dot(cots[:half], wgu, 1, 1), other)

    uh = u * hidden
    ggk = sum(
        jnp.where(hit, jnp.sum(uh[:, i * h : (i + 1) * h], axis=1, keepdims=True), 0.0)
        for i, hit in enumerate(hits)
    )
    gate_grad = scatter(ggk[:half], ggk[half:])

    weight_grad = jnp.stack([gate_part, up_part, down_grad], axis=1)
    weight_grad = weight_grad.reshape(-1, 3, local_experts, h)
    return (layer_out, token_grad, gate_grad, weight_grad)


def solution(mesh):
    experts, groups = mesh.devices.shape
    if (experts, groups) == (8, 4):
        tok = P(("expert", "dp"), None)
        return jax.shard_map(
            fused,
            mesh=mesh,
            in_specs=(tok, tok, tok, P(None, None, "expert", None), tok),
            out_specs=(tok, tok, tok, P("dp", None, "expert", None)),
            check_vma=False,
        )
    split = Mesh(
        mesh.devices.reshape(experts // 2, 2, groups), ("chip", "core", "dp")
    )
    tok = P(("chip", "core", "dp"), None)
    wsp = P(None, None, ("chip", "core"), None)
    return jax.shard_map(
        local,
        mesh=split,
        in_specs=(tok, tok, tok, wsp, tok),
        out_specs=(tok, tok, tok, P("dp", None, ("chip", "core"), None)),
        check_vma=False,
    )
```

```python
import functools
import jax
import jax.numpy as jnp
from jax import lax
from jax.experimental import pallas as pl
from jax.experimental.layout import Layout, with_layout_constraint
from jax.experimental.pallas import tpu as pltpu
from jax.sharding import Mesh, PartitionSpec as P

F32 = jnp.float32
BF16 = jnp.bfloat16
SWAP = [(0, 1), (1, 0)]
META = 16
LANES = 128


def dot(a, b, ca, cb):
    return lax.dot_general(a, b, (((ca,), (cb,)), ((), ())), preferred_element_type=F32)


def place(h, p, j, e):
    return (p * (h // LANES) + j) * 2 + e, (2 * p + e) * h + j * LANES


def fused_kernel(
    tok_ref, og_ref, ids_ref, prob_ref, w_ref,
    lay_ref, tg_ref, gg_ref, acc_ref, buf,
    wv, wst, wf, xg, mb, gu, act, acc, po, ps, pr, rx, ggs,
    loc_sem, w_sem, ld_sem, out_sem,
    xy_s, xy_r, za_s, za_r, zb_s, zb_r, sib_s, sib_r,
    ps_s, ps_r, rx_s, rx_r, gg_s, gg_r, mp_s, mp_r, ml_s, ml_r,
):
    tok, d = tok_ref.shape
    rows = 2 * tok
    hh = wv.shape[1] // 3
    h = hh // 2
    per = 3 * hh // LANES
    step = wf.shape[0] // per
    ch = d // 4
    nt = min(256, hh)
    dt = min(512, d)
    me = lax.axis_index("expert")
    z = lax.axis_index("dp")
    core = me % 2
    xx = (me // 2) % 2
    yy = me // 4

    def peer(m, r):
        return (
            ((yy + m // 2) % 2) * 4 + ((xx + m % 2) % 2) * 2 + (core + r) % 2,
            z,
        )

    xn, yn, sib = peer(1, 0), peer(2, 0), peer(0, 1)
    order = [z, 1 + z % 2, (2 + 3 * z) % 5, 3 - 3 * (z // 2)]

    own_half = tok
    cut_a = rows * 11 // 16 // 16 * 16
    a_half = (cut_a // 2 + 8) // 16 * 16
    h1, h2 = (0, own_half), (own_half, rows - own_half)
    whole, pa, pb = (0, rows), (0, cut_a), (cut_a, rows - cut_a)
    a_rest = cut_a - a_half
    large_first = ((0, a_half), (a_half, a_rest))
    halves = [(h1, h2), large_first, ((0, a_rest), (a_rest, a_half)), large_first]

    def rdma(src, dst, ssem, rsem, dev):
        return pltpu.make_async_remote_copy(
            src_ref=src, dst_ref=dst, send_sem=ssem, recv_sem=rsem,
            device_id=dev, device_id_type=pl.DeviceIdType.MESH,
        )

    def at(r, k, m, part):
        return buf.at[r, k, m, pl.ds(part[0], part[1])]

    def xy(j, i):
        k = order[j]
        p1, p2 = halves[j]
        src, dst, part, dev = [
            (0, 1, p1, xn), (0, 1, p2, xn), (0, 2, p2, yn), (0, 2, p1, yn),
            (1, 3, p1, yn), (2, 3, p2, xn),
        ][i]
        rows_out = at(0, k, src, part)
        if j == 0 and i < 4:
            rows_out = tok_ref if part == h1 else og_ref
        return rdma(rows_out, at(0, k, dst, part), xy_s.at[k, i], xy_r.at[k, i], dev)

    def line(k, m, up):
        dev = (me, z + 1) if up else (me, z - 1)
        u = 1 if up else 0
        if m is None:
            return rdma(at(0, k, 0, pa), at(0, k, 0, pa), za_s.at[k, u], za_r.at[k], dev)
        if m == "meta":
            return rdma(mb.at[k], mb.at[k], ml_s.at[k, u], ml_r.at[k], dev)
        return rdma(at(0, k, m, pb), at(0, k, m, pb), zb_s.at[k, m, u], zb_r.at[k, m], dev)

    def on_line(k, m, what):
        @pl.when((k <= z) & (z < 3))
        def _():
            getattr(line(k, m, True), what)()

        @pl.when((k >= z) & (z > 0))
        def _():
            getattr(line(k, m, False), what)()

    def sibling(k, m, i, part):
        return rdma(at(0, k, m, part), at(1, k, m, part), sib_s.at[k, m, i], sib_r.at[k, m, i], sib)

    own = [
        pltpu.make_async_copy(tok_ref, xg.at[0, 0, pl.ds(0, tok)], loc_sem.at[0]),
        pltpu.make_async_copy(og_ref, xg.at[0, 0, pl.ds(tok, tok)], loc_sem.at[1]),
    ]
    held = pltpu.make_async_copy(xg.at[0, 0], buf.at[0, z, 0], loc_sem.at[2])
    for c in own:
        c.start()
    barrier = pltpu.get_barrier_semaphore()
    for i in range(1, 8):
        pl.semaphore_signal(barrier, inc=1, device_id=peer(i // 2, i % 2), device_id_type=pl.DeviceIdType.MESH)

    @pl.when(z > 0)
    def _():
        pl.semaphore_signal(barrier, inc=1, device_id=(me, z - 1), device_id_type=pl.DeviceIdType.MESH)

    @pl.when(z < 3)
    def _():
        pl.semaphore_signal(barrier, inc=1, device_id=(me, z + 1), device_id_type=pl.DeviceIdType.MESH)

    named = lax.broadcasted_iota(jnp.int32, (META, tok), 0)
    prob = jnp.zeros((META, tok), F32)
    for i in range(ids_ref.shape[0]):
        prob = prob + jnp.where(named == ids_ref[i : i + 1, :], prob_ref[i : i + 1, :], 0.0)
    high = prob.astype(BF16)
    mb[z, 0, :, :tok] = high
    mb[z, 0, :, tok:] = (prob - high.astype(F32)).astype(BF16)
    for c in own:
        c.wait()
    held.start()
    pl.semaphore_wait(barrier, 8 + (z + 1) // 2 % 2)

    def own_first():
        xy(0, 0).start()
        xy(0, 2).start()
        for i in range(1, 8):
            near_meta(i).start()
        held.wait()
        on_line(z, None, "start")

    def own_second():
        xy(0, 1).start()
        xy(0, 3).start()
        sibling(z, 0, 0, whole).start()

    def own_mid(i):
        xy(0, 2 * i).wait_recv()
        xy(0, 4 + i).start()

    def own_near(i):
        xy(0, 1 + 2 * i).wait_recv()
        sibling(z, 1 + i, 0, whole).start()

    def own_far():
        xy(0, 4).wait_recv()
        xy(0, 5).wait_recv()
        sibling(z, 3, 0, whole).start()

    def near_meta(i):
        return rdma(mb.at[z, 0], mb.at[z, i], mp_s.at[i], mp_r.at[i], peer(i // 2, i % 2))

    def metas():
        for i in range(1, 8):
            near_meta(i).wait_recv()
        on_line(z, "meta", "start")

    def wave(n, m):
        @pl.when(z + n <= 3)
        def _():
            take(z + n, m)

            @pl.when(z > 0)
            def _():
                line(z + n, m, False).start()

        @pl.when(z - n >= 0)
        def _():
            take(z - n, m)

            @pl.when(z < 3)
            def _():
                line(z - n, m, True).start()

    def take(k, m):
        line(k, m, True).wait_recv()
        if m is None:
            sibling(k, 0, 0, pa).start()
        elif m != "meta":
            sibling(k, m, 1, pb).start()

    def far_out(j, i):
        xy(j, i).start()
        xy(j, (2, 3)[i]).start()

    def far_mid(j, i):
        xy(j, 2 * i).wait_recv()
        xy(j, 4 + i).start()

    def far_near(j, i):
        xy(j, 1 + 2 * i).wait_recv()
        sibling(order[j], 1 + i, 0, pa).start()

    def far_far(j):
        xy(j, 4).wait_recv()
        xy(j, 5).wait_recv()
        sibling(order[j], 3, 0, pa).start()

    def raw(c):
        return pltpu.make_async_copy(
            w_ref.at[pl.ds(pl.multiple_of(c * step * per, step * per), step * per)],
            wst.at[c % 2], w_sem.at[c % 2],
        )

    def lay_weights():
        n = d // step
        raw(0).start()

        def chunk(c, carry):
            @pl.when(c + 1 < n)
            def _():
                raw(c + 1).start()

            raw(c).wait()
            wf[...] = wst[c % 2].astype(F32)
            to = pl.ds(pl.multiple_of(c * step, step), step)
            for p in range(3):
                for j in range(h // LANES):
                    for e in range(2):
                        at_row, col = place(h, p, j, e)
                        wv[to, col : col + LANES] = wf[pl.ds(at_row, step, stride=per), :].astype(BF16)
            return carry

        lax.fori_loop(0, n, chunk, 0)

    def load(k, s, i, what, blocks=range(4)):
        for b in blocks:
            part = pl.ds(i * tok, tok)
            c = pltpu.make_async_copy(
                buf.at[b % 2, k, 2 * s + b // 2, part], xg.at[s, b, part], ld_sem.at[s, b, i]
            )
            getattr(c, what)()

    def load_x(k, s, mine):
        for m in (2 * s, 2 * s + 1):
            sibling(k, m, 0, whole if mine else pa).wait_recv()
        load(k, s, 0, "start")

    def load_g(k, s, mine, blocks=range(4)):
        if not mine:
            for b in blocks[::2]:
                sibling(k, 2 * s + b // 2, 1, pb).wait_recv()
        load(k, s, 1, "start", blocks)

    def gates(k, s):
        load(k, s, 0, "wait")

        def tile(n, carry):
            c0 = pl.multiple_of(n * nt, nt)
            xs = xg[s, :, 0:tok, :].reshape(4 * tok, d)
            for i in range(2):
                gu[s, i, :, pl.ds(c0, nt)] = dot(xs, wv[:, pl.ds(i * hh + c0, nt)], 1, 0)
            return carry

        lax.fori_loop(0, hh // nt, tile, 0)

    def hidden_cots(k, s, mine, blocks=range(4)):
        load(k, s, 1, "wait", blocks)
        b0, b1, n_rows = blocks[0], blocks[-1] + 1, len(blocks) * tok
        span = slice(b0 * tok, b1 * tok)

        def tile(n, gg):
            c0 = pl.multiple_of(n * nt, nt)
            gs = xg[s, b0:b1, tok:, :].reshape(n_rows, d)
            u = dot(gs, wv[:, pl.ds(2 * hh + c0, nt)], 1, 0)
            gate = gu[s, 0, span, pl.ds(c0, nt)]
            up = gu[s, 1, span, pl.ds(c0, nt)]
            col = c0 + lax.broadcasted_iota(jnp.int32, (2 * META, nt), 1)
            row = lax.broadcasted_iota(jnp.int32, (2 * META, nt), 0) % META
            sel = (row == 2 * me + (col >= h).astype(jnp.int32)).astype(F32).astype(BF16)
            shares = []
            for b in blocks:
                both = jnp.concatenate(
                    [mb[k, 4 * s + b, :, :tok], mb[k, 4 * s + b, :, tok:]], axis=0
                )
                shares.append(dot(both, sel, 0, 0))
            p = jnp.concatenate(shares, axis=0)
            sig = jax.nn.sigmoid(gate)
            silu = gate * sig
            hidden = silu * up
            hc = p * u
            act[span, pl.ds(c0, nt)] = (hc * up * (sig + silu * (1.0 - sig))).astype(BF16)
            act[span, pl.ds(hh + c0, nt)] = (hc * silu).astype(BF16)
            act[span, pl.ds(2 * hh + c0, nt)] = (p * hidden).astype(BF16)
            if mine:
                uh = u * hidden
                hi = uh.astype(BF16)
                lo = (uh - hi.astype(F32)).astype(BF16)
                own_row = lax.broadcasted_iota(jnp.int32, (8, nt), 0)
                own_col = c0 + lax.broadcasted_iota(jnp.int32, (8, nt), 1)
                pick = (own_row == (own_col >= h).astype(jnp.int32)).astype(F32).astype(BF16)
                gg = gg + dot(pick, hi, 1, 1) + dot(pick, lo, 1, 1)
            return gg

        start = jnp.zeros((8, 4 * tok), F32)
        gg = lax.fori_loop(0, hh // nt, tile, start)
        if mine:
            for b in range(4):
                ggs[4 * s + b] = gg[:, b * tok : (b + 1) * tok]

    def third(s, blocks=range(4), last=False):
        x0 = pl.multiple_of(z * ch, ch)
        b0, b1, n_rows = blocks[0], blocks[-1] + 1, len(blocks) * tok
        span = slice(b0 * tok, b1 * tok)
        cuts = ((0, hh), (hh, hh), (2 * hh, hh)) if last else ((0, 2 * hh), (2 * hh, hh))
        for i, (c0, width) in enumerate(cuts):
            top = tok if c0 == 2 * hh else 0
            rows_in = xg[s, b0:b1, top : top + tok, pl.ds(x0, ch)].reshape(n_rows, ch)
            acc[:, c0 : c0 + width] += dot(rows_in, act[span, c0 : c0 + width], 0, 0)
            if last:
                grads_out(i).start()

    def grads_out(i):
        part = pl.ds(i * hh, hh)
        return pltpu.make_async_copy(acc.at[:, part], acc_ref.at[:, part], out_sem.at[i])

    def second(s):
        def tile(n, carry):
            r0 = pl.multiple_of(n * dt, dt)
            out = dot(act[:, 2 * hh :], wv[pl.ds(r0, dt), 2 * hh :], 1, 1).astype(BF16)
            tg = dot(act[:, : 2 * hh], wv[pl.ds(r0, dt), : 2 * hh], 1, 1).astype(BF16)
            for mi in range(2):
                for q, v in ((0, out), (1, tg)):
                    b = 2 * mi * tok
                    po[q, 2 * s + mi, :, pl.ds(r0, dt)] = v[b : b + tok]
                    ps[q, 2 * s + mi, :, pl.ds(r0, dt)] = v[b + tok : b + 2 * tok]
            return carry

        lax.fori_loop(0, d // dt, tile, 0)

    def swap(q, s):
        part = pl.ds(2 * s, 2)
        return rdma(ps.at[q, part], pr.at[q, part], ps_s.at[q, s], ps_r.at[q, s], sib)

    def add(i, j):
        po[i] = (po[i].astype(F32) + j.astype(F32)).astype(BF16)

    def merge(s):
        for q in range(2):
            swap(q, s).wait_recv()
            for m in (2 * s, 2 * s + 1):
                add((q, m), pr[q, m])

    def back(q, i):
        near, far = (1, 2) if q == 0 else (2, 1)
        dev, dev2 = (xn, yn) if q == 0 else (yn, xn)
        if i < 2:
            return rdma(po.at[q, (near, 3)[i]], rx.at[q, i], rx_s.at[q, i], rx_r.at[q, i], dev)
        return rdma(po.at[q, far], rx.at[q, 2], rx_s.at[q, 2], rx_r.at[q, 2], dev2)

    def back_mid(q):
        far = 2 if q == 0 else 1
        back(q, 1).wait_recv()
        add((q, far), rx[q, 1])
        back(q, 2).start()

    def back_end(q, ref):
        back(q, 0).wait_recv()
        back(q, 2).wait_recv()
        ref[...] = (po[q, 0].astype(F32) + rx[q, 0].astype(F32) + rx[q, 2].astype(F32)).astype(BF16)

    def gg_copy(i):
        return rdma(ggs.at[i], gg_ref.at[i], gg_s.at[i], gg_r.at[i], peer(i // 2, i % 2))

    k1, k2, k3 = order[1:]
    own_first()
    own_second()
    acc[...] = jnp.zeros_like(acc)
    lay_weights()
    wave(1, None)
    own_mid(1)
    own_near(1)
    own_mid(0)
    own_near(0)
    load_x(z, 0, True)
    metas()
    on_line(z, 0, "start")
    far_out(1, 0)
    own_far()
    wave(2, None)
    far_out(2, 0)
    far_out(1, 1)
    gates(z, 0)
    far_mid(1, 0)
    load_x(z, 1, True)
    on_line(z, 1, "start")
    on_line(z, 2, "start")
    load_g(z, 0, True)
    hidden_cots(z, 0, True)
    far_out(2, 1)
    load_g(z, 1, True)
    far_mid(2, 0)
    far_mid(1, 1)
    second(0)
    swap(0, 0).start()
    swap(1, 0).start()
    third(0)
    far_near(1, 0)
    gates(z, 1)
    wave(1, 0)
    wave(1, "meta")
    hidden_cots(z, 1, True)
    far_mid(2, 1)
    load_x(k1, 0, False)
    wave(3, None)
    far_near(1, 1)
    wave(1, 1)
    second(1)
    swap(0, 1).start()
    swap(1, 1).start()
    for i in range(1, 8):
        gg_copy(i).start()
    gg_ref[0] = ggs[0]
    far_out(3, 0)
    far_far(1)
    gates(k1, 0)
    on_line(z, 3, "start")
    far_mid(3, 1)
    wave(1, 2)
    merge(0)
    far_near(2, 1)
    load_g(k1, 0, False)
    far_out(3, 1)
    third(1)
    far_near(2, 0)
    hidden_cots(k1, 0, False)
    far_mid(3, 0)
    merge(1)
    wave(2, 0)
    wave(2, "meta")
    third(0)
    far_far(2)
    wave(1, 3)
    load_x(k2, 0, False)
    gates(k2, 0)
    load_x(k1, 1, False)
    far_near(3, 0)
    back(0, 1).start()
    back(0, 0).start()
    back(1, 1).start()
    back(1, 0).start()
    wave(2, 1)
    load_g(k1, 1, False)
    gates(k1, 1)
    hidden_cots(k1, 1, False)
    load_g(k2, 0, False)
    third(1)
    wave(2, 2)
    load_x(k2, 1, False)
    far_near(3, 1)
    hidden_cots(k2, 0, False)
    far_far(3)
    gates(k2, 1)
    wave(3, 0)
    wave(3, "meta")
    third(0)
    load_x(k3, 0, False)
    wave(2, 3)
    load_g(k2, 1, False)
    hidden_cots(k2, 1, False)
    wave(3, 1)
    gates(k3, 0)
    load_g(k3, 0, False)
    back_mid(1)
    third(1)
    back_mid(0)
    wave(3, 2)
    hidden_cots(k3, 0, False)
    load_x(k3, 1, False)
    third(0)
    wave(3, 3)
    load_g(k3, 1, False, range(0, 2))
    gates(k3, 1)
    load_g(k3, 1, False, range(2, 4))
    hidden_cots(k3, 1, False, range(0, 2))
    third(1, range(0, 2))
    hidden_cots(k3, 1, False, range(2, 4))
    back_end(1, tg_ref)
    third(1, range(2, 4), True)
    back_end(0, lay_ref)

    for i in range(3):
        grads_out(i).wait()
    for j in range(4):
        for i in range(6):
            xy(j, i).wait_send()
    for m in range(4):
        sibling(z, m, 0, whole).wait_send()
    for k in (k1, k2, k3):
        for m in range(4):
            sibling(k, m, 0, pa).wait_send()
            sibling(k, m, 1, pb).wait_send()
    for k in order:
        on_line(k, None, "wait_send")
        on_line(k, "meta", "wait_send")
        for m in range(4):
            on_line(k, m, "wait_send")
    for q in range(2):
        for s in range(2):
            swap(q, s).wait_send()
        for i in range(3):
            back(q, i).wait_send()
    for i in range(1, 8):
        gg_copy(i).wait_recv()
        gg_copy(i).wait_send()
        near_meta(i).wait_send()


def finish_kernel(acc_ref, lay_ref, tg_ref, gg_ref, ids_ref, wg_out, lay_out, tg_out, gate_out):
    rows, cols = acc_ref.shape
    h = cols // 6
    for p in range(3):
        for j in range(h // LANES):
            for e in range(2):
                at_row, col = place(h, p, j, e)
                wg_out[pl.ds(at_row, rows, stride=cols // LANES), :] = acc_ref[:, col : col + LANES]
    lay_out[...] = lay_ref[...]
    tg_out[...] = tg_ref[...]

    @pl.when(pl.program_id(0) == 0)
    def _():
        me = lax.axis_index("expert")
        ids = ids_ref[...]
        total = jnp.zeros(ids.shape, F32)
        for i in range(8):
            source = (
                (me // 4 + i // 4) % 2 * 4 + (me // 2 + i // 2) % 2 * 2 + (me + i) % 2
            )
            for e in range(2):
                total = total + jnp.where(ids == 2 * source + e, gg_ref[i, e : e + 1, :], 0.0)
        gate_out[...] = total


def finish(acc, lay, tg, gg, ids):
    rows, cols = acc.shape
    n = 8
    per = cols // LANES
    tall = pl.BlockSpec((rows // n, cols), lambda i: (i, 0))
    wide = pl.BlockSpec((lay.shape[0] // n, lay.shape[1]), lambda i: (i, 0))
    flat = pl.BlockSpec(ids.shape, lambda i: (0, 0))
    return pl.pallas_call(
        finish_kernel,
        grid=(n,),
        out_shape=[
            jax.ShapeDtypeStruct((rows * per, LANES), F32),
            jax.ShapeDtypeStruct(lay.shape, lay.dtype),
            jax.ShapeDtypeStruct(tg.shape, tg.dtype),
            jax.ShapeDtypeStruct(ids.shape, F32),
        ],
        in_specs=[tall, wide, wide, pl.BlockSpec(gg.shape, lambda i: (0, 0, 0)), flat],
        out_specs=[pl.BlockSpec((rows // n * per, LANES), lambda i: (i, 0)), wide, wide, flat],
        compiler_params=pltpu.CompilerParams(vmem_limit_bytes=60 * 1024 * 1024),
    )(acc, lay, tg, gg, ids)


def fused(tokens, expert_ids, gate_probs, expert_weights, out_grad):
    tok, top = expert_ids.shape
    d = tokens.shape[1]
    local_experts, h = expert_weights.shape[2:]
    hh = local_experts * h
    rows = 2 * tok
    ids = expert_ids.T

    w = with_layout_constraint(
        expert_weights.reshape(d, 3, local_experts, h // LANES, LANES),
        Layout(major_to_minor=(0, 1, 3, 2, 4)),
    )
    per = 3 * hh // LANES
    w = jnp.transpose(w, (0, 1, 3, 2, 4)).reshape(d * per, LANES)
    step = 128

    any_ = pl.BlockSpec(memory_space=pl.ANY)
    vmem = pl.BlockSpec(memory_space=pltpu.VMEM)
    dma = pltpu.SemaphoreType.DMA
    lay, tg, gg, acc, _ = pl.pallas_call(
        fused_kernel,
        out_shape=[
            jax.ShapeDtypeStruct((tok, d), BF16),
            jax.ShapeDtypeStruct((tok, d), BF16),
            jax.ShapeDtypeStruct((8, 8, tok), F32),
            jax.ShapeDtypeStruct((d // 4, 3 * hh), F32),
            jax.ShapeDtypeStruct((2, 4, 4, rows, d), BF16),
        ],
        in_specs=[any_, any_, vmem, vmem, any_],
        out_specs=[vmem, vmem, vmem, any_, any_],
        scratch_shapes=[
            pltpu.VMEM((d, 3 * hh), BF16),
            pltpu.VMEM((2, step * per, LANES), BF16),
            pltpu.VMEM((step * per, LANES), F32),
            pltpu.VMEM((2, 4, rows, d), BF16),
            pltpu.VMEM((4, 8, META, 2 * tok), BF16),
            pltpu.VMEM((2, 2, 4 * tok, hh), F32),
            pltpu.VMEM((4 * tok, 3 * hh), BF16),
            pltpu.VMEM((d // 4, 3 * hh), F32),
            pltpu.VMEM((2, 4, tok, d), BF16),
            pltpu.VMEM((2, 4, tok, d), BF16),
            pltpu.VMEM((2, 4, tok, d), BF16),
            pltpu.VMEM((2, 3, tok, d), BF16),
            pltpu.VMEM((8, 8, tok), F32),
            dma((3,)), dma((2,)), dma((2, 4, 2)), dma((3,)),
            dma((4, 6)), dma((4, 6)), dma((4, 2)), dma((4,)),
            dma((4, 4, 2)), dma((4, 4)), dma((4, 4, 2)), dma((4, 4, 2)),
            dma((2, 2)), dma((2, 2)), dma((2, 3)), dma((2, 3)), dma((8,)), dma((8,)),
            dma((8,)), dma((8,)), dma((4, 2)), dma((4,)),
        ],
        compiler_params=pltpu.CompilerParams(
            collective_id=0, has_side_effects=True, vmem_limit_bytes=60 * 1024 * 1024
        ),
    )(tokens, out_grad, ids, gate_probs.T, w)

    wg, lay, tg, gate_grad = finish(acc, lay, tg, gg, ids)
    wg = jnp.transpose(wg.reshape(d // 4, 3, h // LANES, local_experts, LANES), (0, 1, 3, 2, 4))
    wg = with_layout_constraint(wg, Layout(major_to_minor=(0, 1, 3, 2, 4)))
    return lay, tg, gate_grad.T, wg.reshape(d // 4, 3, local_experts, h)


def gather(rows):
    n = lax.axis_size("chip")
    own = [rows] + [
        lax.ppermute(rows, "chip", [(i, i ^ k) for i in range(n)]) for k in range(1, n)
    ]
    own = jnp.concatenate(own, axis=0)
    return jnp.concatenate([own, lax.ppermute(own, "core", SWAP)], axis=0)


def scatter(own, other):
    n = lax.axis_size("chip")
    me = lax.axis_index("chip")
    total = own + lax.ppermute(other, "core", SWAP).astype(F32)
    total = total.astype(other.dtype).reshape((n, -1) + own.shape[1:])
    total = jnp.concatenate(
        [lax.dynamic_index_in_dim(total, me ^ k, 0, keepdims=False) for k in range(n)],
        axis=0,
    )
    return lax.psum_scatter(total, "chip", scatter_dimension=0, tiled=True)


def line_scatter(grad):
    n = lax.axis_size("dp")
    me = lax.axis_index("dp")
    rows = grad.shape[0] // n

    def chunk(i):
        i = jnp.clip(i, 0, n - 1)
        return lax.dynamic_slice_in_dim(grad, i * rows, rows, 0).astype(F32)

    up = down = None
    for t in range(n - 1):
        a = chunk(n - 1 - t + me)
        b = chunk(t - (n - 1) + me)
        if t:
            a = a + up.astype(F32)
            b = b + down.astype(F32)
        up = lax.ppermute(a.astype(BF16), "dp", [(i, i + 1) for i in range(t + 1)])
        down = lax.ppermute(
            b.astype(BF16), "dp", [(i, i - 1) for i in range(n - 1 - t, n)]
        )
    return chunk(me) + up.astype(F32) + down.astype(F32)


def local(tokens, expert_ids, gate_probs, expert_weights, out_grad):
    tok_count, top_count = expert_ids.shape
    d = tokens.shape[1]
    chips = lax.axis_size("chip")
    me = lax.axis_index("chip") * 2 + lax.axis_index("core")
    local_experts, h = expert_weights.shape[2:]
    half = chips * tok_count
    eh = local_experts * h

    x = gather(tokens)
    small = gather(jnp.concatenate([expert_ids.astype(F32), gate_probs], axis=1))
    g = gather(out_grad)
    ids = small[:, :top_count].astype(jnp.int32)
    probs = small[:, top_count:]

    hits = [ids == me * local_experts + i for i in range(local_experts)]
    p = jnp.concatenate(
        [
            jnp.broadcast_to(
                jnp.sum(jnp.where(hit, probs, 0.0), axis=1, keepdims=True), (2 * half, h)
            )
            for hit in hits
        ],
        axis=1,
    )

    w = expert_weights.reshape(d, 3 * eh)
    wgu = w[:, : 2 * eh]
    wd = w[:, 2 * eh :]

    a = dot(x, wgu, 1, 0)
    gate = a[:, :eh]
    up = a[:, eh:]
    s = jax.nn.sigmoid(gate)
    hidden = gate * s * up
    ph = (p * hidden).astype(BF16)
    down_grad = line_scatter(dot(g, ph, 0, 0).astype(BF16))

    u = dot(g, wd, 1, 0)
    hc = p * u
    gc = (hc * up * s * (1.0 + gate * (1.0 - s))).astype(BF16)
    uc = (hc * gate * s).astype(BF16)
    gate_part = line_scatter(dot(x, gc, 0, 0).astype(BF16))
    up_part = line_scatter(dot(x, uc, 0, 0).astype(BF16))

    other = dot(ph[half:], wd, 1, 1).astype(BF16)
    layer_out = scatter(dot(ph[:half], wd, 1, 1), other)

    cots = jnp.concatenate([gc, uc], axis=1)
    other = dot(cots[half:], wgu, 1, 1).astype(BF16)
    token_grad = scatter(dot(cots[:half], wgu, 1, 1), other)

    uh = u * hidden
    ggk = sum(
        jnp.where(hit, jnp.sum(uh[:, i * h : (i + 1) * h], axis=1, keepdims=True), 0.0)
        for i, hit in enumerate(hits)
    )
    gate_grad = scatter(ggk[:half], ggk[half:])

    weight_grad = jnp.stack([gate_part, up_part, down_grad], axis=1)
    weight_grad = weight_grad.reshape(-1, 3, local_experts, h)
    return (layer_out, token_grad, gate_grad, weight_grad)


def solution(mesh):
    experts, groups = mesh.devices.shape
    if (experts, groups) == (8, 4):
        tok = P(("expert", "dp"), None)
        return jax.shard_map(
            fused,
            mesh=mesh,
            in_specs=(tok, tok, tok, P(None, None, "expert", None), tok),
            out_specs=(tok, tok, tok, P("dp", None, "expert", None)),
            check_vma=False,
        )
    split = Mesh(
        mesh.devices.reshape(experts // 2, 2, groups), ("chip", "core", "dp")
    )
    tok = P(("chip", "core", "dp"), None)
    wsp = P(None, None, ("chip", "core"), None)
    return jax.shard_map(
        local,
        mesh=split,
        in_specs=(tok, tok, tok, wsp, tok),
        out_specs=(tok, tok, tok, P("dp", None, ("chip", "core"), None)),
        check_vma=False,
    )
```

```python
import functools
import jax
import jax.numpy as jnp
from jax import lax
from jax.experimental import pallas as pl
from jax.experimental.layout import Layout, with_layout_constraint
from jax.experimental.pallas import tpu as pltpu
from jax.sharding import Mesh, PartitionSpec as P

F32 = jnp.float32
BF16 = jnp.bfloat16
SWAP = [(0, 1), (1, 0)]
META = 16
LANES = 128


def dot(a, b, ca, cb):
    return lax.dot_general(a, b, (((ca,), (cb,)), ((), ())), preferred_element_type=F32)


def place(h, p, j, e):
    return (p * (h // LANES) + j) * 2 + e, (2 * p + e) * h + j * LANES


def fused_kernel(
    tok_ref, og_ref, ids_ref, prob_ref, w_ref,
    lay_ref, tg_ref, gg_ref, acc_ref, buf,
    wv, wst, wf, xg, mb, gu, act, acc, po, ps, pr, rx, ggs,
    loc_sem, w_sem, ld_sem, out_sem,
    xy_s, xy_r, za_s, za_r, zb_s, zb_r, sib_s, sib_r,
    ps_s, ps_r, rx_s, rx_r, gg_s, gg_r, mp_s, mp_r, ml_s, ml_r,
):
    tok, d = tok_ref.shape
    rows = 2 * tok
    hh = wv.shape[1] // 3
    h = hh // 2
    per = 3 * hh // LANES
    step = wf.shape[0] // per
    ch = d // 4
    nt = min(256, hh)
    dt = min(512, d)
    me = lax.axis_index("expert")
    z = lax.axis_index("dp")
    core = me % 2
    xx = (me // 2) % 2
    yy = me // 4

    def peer(m, r):
        return (
            ((yy + m // 2) % 2) * 4 + ((xx + m % 2) % 2) * 2 + (core + r) % 2,
            z,
        )

    xn, yn, sib = peer(1, 0), peer(2, 0), peer(0, 1)
    order = [z, 1 + z % 2, (2 + 3 * z) % 5, 3 - 3 * (z // 2)]

    own_half = tok
    cut_a = rows * 11 // 16 // 16 * 16
    a_half = (cut_a // 2 + 8) // 16 * 16
    h1, h2 = (0, own_half), (own_half, rows - own_half)
    whole, pa, pb = (0, rows), (0, cut_a), (cut_a, rows - cut_a)
    a_rest = cut_a - a_half
    large_first = ((0, a_half), (a_half, a_rest))
    halves = [(h1, h2), large_first, ((0, a_rest), (a_rest, a_half)), large_first]

    def rdma(src, dst, ssem, rsem, dev):
        return pltpu.make_async_remote_copy(
            src_ref=src, dst_ref=dst, send_sem=ssem, recv_sem=rsem,
            device_id=dev, device_id_type=pl.DeviceIdType.MESH,
        )

    def at(r, k, m, part):
        return buf.at[r, k, m, pl.ds(part[0], part[1])]

    def xy(j, i):
        k = order[j]
        p1, p2 = halves[j]
        src, dst, part, dev = [
            (0, 1, p1, xn), (0, 1, p2, xn), (0, 2, p2, yn), (0, 2, p1, yn),
            (1, 3, p1, yn), (2, 3, p2, xn),
        ][i]
        rows_out = at(0, k, src, part)
        if j == 0 and i < 4:
            rows_out = tok_ref if part == h1 else og_ref
        return rdma(rows_out, at(0, k, dst, part), xy_s.at[k, i], xy_r.at[k, i], dev)

    def line(k, m, up):
        dev = (me, z + 1) if up else (me, z - 1)
        u = 1 if up else 0
        if m is None:
            return rdma(at(0, k, 0, pa), at(0, k, 0, pa), za_s.at[k, u], za_r.at[k], dev)
        if m == "meta":
            return rdma(mb.at[k], mb.at[k], ml_s.at[k, u], ml_r.at[k], dev)
        return rdma(at(0, k, m, pb), at(0, k, m, pb), zb_s.at[k, m, u], zb_r.at[k, m], dev)

    def on_line(k, m, what):
        @pl.when((k <= z) & (z < 3))
        def _():
            getattr(line(k, m, True), what)()

        @pl.when((k >= z) & (z > 0))
        def _():
            getattr(line(k, m, False), what)()

    def sibling(k, m, i, part):
        return rdma(at(0, k, m, part), at(1, k, m, part), sib_s.at[k, m, i], sib_r.at[k, m, i], sib)

    own = [
        pltpu.make_async_copy(tok_ref, xg.at[0, 0, pl.ds(0, tok)], loc_sem.at[0]),
        pltpu.make_async_copy(og_ref, xg.at[0, 0, pl.ds(tok, tok)], loc_sem.at[1]),
    ]
    held = pltpu.make_async_copy(xg.at[0, 0], buf.at[0, z, 0], loc_sem.at[2])
    for c in own:
        c.start()
    barrier = pltpu.get_barrier_semaphore()
    for i in range(1, 8):
        pl.semaphore_signal(barrier, inc=1, device_id=peer(i // 2, i % 2), device_id_type=pl.DeviceIdType.MESH)

    @pl.when(z > 0)
    def _():
        pl.semaphore_signal(barrier, inc=1, device_id=(me, z - 1), device_id_type=pl.DeviceIdType.MESH)

    @pl.when(z < 3)
    def _():
        pl.semaphore_signal(barrier, inc=1, device_id=(me, z + 1), device_id_type=pl.DeviceIdType.MESH)

    named = lax.broadcasted_iota(jnp.int32, (META, tok), 0)
    prob = jnp.zeros((META, tok), F32)
    for i in range(ids_ref.shape[0]):
        prob = prob + jnp.where(named == ids_ref[i : i + 1, :], prob_ref[i : i + 1, :], 0.0)
    high = prob.astype(BF16)
    mb[z, 0, :, :tok] = high
    mb[z, 0, :, tok:] = (prob - high.astype(F32)).astype(BF16)
    for c in own:
        c.wait()
    held.start()
    pl.semaphore_wait(barrier, 8 + (z + 1) // 2 % 2)

    def own_first():
        xy(0, 0).start()
        xy(0, 2).start()
        for i in range(1, 8):
            near_meta(i).start()
        held.wait()
        on_line(z, None, "start")

    def own_second():
        xy(0, 1).start()
        xy(0, 3).start()
        sibling(z, 0, 0, whole).start()

    def own_mid(i):
        xy(0, 2 * i).wait_recv()
        xy(0, 4 + i).start()

    def own_near(i):
        xy(0, 1 + 2 * i).wait_recv()
        sibling(z, 1 + i, 0, whole).start()

    def own_far():
        xy(0, 4).wait_recv()
        xy(0, 5).wait_recv()
        sibling(z, 3, 0, whole).start()

    def near_meta(i):
        return rdma(mb.at[z, 0], mb.at[z, i], mp_s.at[i], mp_r.at[i], peer(i // 2, i % 2))

    def metas():
        for i in range(1, 8):
            near_meta(i).wait_recv()
        on_line(z, "meta", "start")

    def wave(n, m):
        @pl.when(z + n <= 3)
        def _():
            take(z + n, m)

            @pl.when(z > 0)
            def _():
                line(z + n, m, False).start()

        @pl.when(z - n >= 0)
        def _():
            take(z - n, m)

            @pl.when(z < 3)
            def _():
                line(z - n, m, True).start()

    def take(k, m):
        line(k, m, True).wait_recv()
        if m is None:
            sibling(k, 0, 0, pa).start()
        elif m != "meta":
            sibling(k, m, 1, pb).start()

    def far_out(j, i):
        xy(j, i).start()
        xy(j, (2, 3)[i]).start()

    def far_mid(j, i):
        xy(j, 2 * i).wait_recv()
        xy(j, 4 + i).start()

    def far_near(j, i):
        xy(j, 1 + 2 * i).wait_recv()
        sibling(order[j], 1 + i, 0, pa).start()

    def far_far(j):
        xy(j, 4).wait_recv()
        xy(j, 5).wait_recv()
        sibling(order[j], 3, 0, pa).start()

    def raw(c):
        return pltpu.make_async_copy(
            w_ref.at[pl.ds(pl.multiple_of(c * step * per, step * per), step * per)],
            wst.at[c % 2], w_sem.at[c % 2],
        )

    def lay_weights():
        n = d // step
        raw(0).start()

        def chunk(c, carry):
            @pl.when(c + 1 < n)
            def _():
                raw(c + 1).start()

            raw(c).wait()
            wf[...] = wst[c % 2].astype(F32)
            to = pl.ds(pl.multiple_of(c * step, step), step)
            for p in range(3):
                for j in range(h // LANES):
                    for e in range(2):
                        at_row, col = place(h, p, j, e)
                        wv[to, col : col + LANES] = wf[pl.ds(at_row, step, stride=per), :].astype(BF16)
            return carry

        lax.fori_loop(0, n, chunk, 0)

    def load(k, s, i, what, blocks=range(4)):
        for b in blocks:
            part = pl.ds(i * tok, tok)
            c = pltpu.make_async_copy(
                buf.at[b % 2, k, 2 * s + b // 2, part], xg.at[s, b, part], ld_sem.at[s, b, i]
            )
            getattr(c, what)()

    def load_x(k, s, mine):
        for m in (2 * s, 2 * s + 1):
            sibling(k, m, 0, whole if mine else pa).wait_recv()
        load(k, s, 0, "start")

    def load_g(k, s, mine, blocks=range(4)):
        if not mine:
            for b in blocks[::2]:
                sibling(k, 2 * s + b // 2, 1, pb).wait_recv()
        load(k, s, 1, "start", blocks)

    def gates(k, s):
        load(k, s, 0, "wait")

        def tile(n, carry):
            c0 = pl.multiple_of(n * nt, nt)
            xs = xg[s, :, 0:tok, :].reshape(4 * tok, d)
            for i in range(2):
                gu[s, i, :, pl.ds(c0, nt)] = dot(xs, wv[:, pl.ds(i * hh + c0, nt)], 1, 0)
            return carry

        lax.fori_loop(0, hh // nt, tile, 0)

    def hidden_cots(k, s, mine, blocks=range(4)):
        load(k, s, 1, "wait", blocks)
        b0, b1, n_rows = blocks[0], blocks[-1] + 1, len(blocks) * tok
        span = slice(b0 * tok, b1 * tok)

        def tile(n, gg):
            c0 = pl.multiple_of(n * nt, nt)
            gs = xg[s, b0:b1, tok:, :].reshape(n_rows, d)
            u = dot(gs, wv[:, pl.ds(2 * hh + c0, nt)], 1, 0)
            gate = gu[s, 0, span, pl.ds(c0, nt)]
            up = gu[s, 1, span, pl.ds(c0, nt)]
            col = c0 + lax.broadcasted_iota(jnp.int32, (2 * META, nt), 1)
            row = lax.broadcasted_iota(jnp.int32, (2 * META, nt), 0) % META
            sel = (row == 2 * me + (col >= h).astype(jnp.int32)).astype(F32).astype(BF16)
            shares = []
            for b in blocks:
                both = jnp.concatenate(
                    [mb[k, 4 * s + b, :, :tok], mb[k, 4 * s + b, :, tok:]], axis=0
                )
                shares.append(dot(both, sel, 0, 0))
            p = jnp.concatenate(shares, axis=0)
            sig = jax.nn.sigmoid(gate)
            silu = gate * sig
            hidden = silu * up
            hc = p * u
            act[span, pl.ds(c0, nt)] = (hc * up * (sig + silu * (1.0 - sig))).astype(BF16)
            act[span, pl.ds(hh + c0, nt)] = (hc * silu).astype(BF16)
            act[span, pl.ds(2 * hh + c0, nt)] = (p * hidden).astype(BF16)
            if mine:
                uh = u * hidden
                hi = uh.astype(BF16)
                lo = (uh - hi.astype(F32)).astype(BF16)
                own_row = lax.broadcasted_iota(jnp.int32, (8, nt), 0)
                own_col = c0 + lax.broadcasted_iota(jnp.int32, (8, nt), 1)
                pick = (own_row == (own_col >= h).astype(jnp.int32)).astype(F32).astype(BF16)
                gg = gg + dot(pick, hi, 1, 1) + dot(pick, lo, 1, 1)
            return gg

        start = jnp.zeros((8, 4 * tok), F32)
        gg = lax.fori_loop(0, hh // nt, tile, start)
        if mine:
            for b in range(4):
                ggs[4 * s + b] = gg[:, b * tok : (b + 1) * tok]

    def third(s, blocks=range(4), last=False):
        x0 = pl.multiple_of(z * ch, ch)
        b0, b1, n_rows = blocks[0], blocks[-1] + 1, len(blocks) * tok
        span = slice(b0 * tok, b1 * tok)
        cuts = ((0, hh), (hh, hh), (2 * hh, hh)) if last else ((0, 2 * hh), (2 * hh, hh))
        for i, (c0, width) in enumerate(cuts):
            top = tok if c0 == 2 * hh else 0
            rows_in = xg[s, b0:b1, top : top + tok, pl.ds(x0, ch)].reshape(n_rows, ch)
            acc[:, c0 : c0 + width] += dot(rows_in, act[span, c0 : c0 + width], 0, 0)
            if last:
                grads_out(i).start()

    def grads_out(i):
        part = pl.ds(i * hh, hh)
        return pltpu.make_async_copy(acc.at[:, part], acc_ref.at[:, part], out_sem.at[i])

    def second(s):
        def tile(n, carry):
            r0 = pl.multiple_of(n * dt, dt)
            out = dot(act[:, 2 * hh :], wv[pl.ds(r0, dt), 2 * hh :], 1, 1).astype(BF16)
            tg = dot(act[:, : 2 * hh], wv[pl.ds(r0, dt), : 2 * hh], 1, 1).astype(BF16)
            for mi in range(2):
                for q, v in ((0, out), (1, tg)):
                    b = 2 * mi * tok
                    po[q, 2 * s + mi, :, pl.ds(r0, dt)] = v[b : b + tok]
                    ps[q, 2 * s + mi, :, pl.ds(r0, dt)] = v[b + tok : b + 2 * tok]
            return carry

        lax.fori_loop(0, d // dt, tile, 0)

    def swap(q, s):
        part = pl.ds(2 * s, 2)
        return rdma(ps.at[q, part], pr.at[q, part], ps_s.at[q, s], ps_r.at[q, s], sib)

    def add(i, j):
        po[i] = (po[i].astype(F32) + j.astype(F32)).astype(BF16)

    def merge(s):
        for q in range(2):
            swap(q, s).wait_recv()
            for m in (2 * s, 2 * s + 1):
                add((q, m), pr[q, m])

    def back(q, i):
        near, far = (1, 2) if q == 0 else (2, 1)
        dev, dev2 = (xn, yn) if q == 0 else (yn, xn)
        if i < 2:
            return rdma(po.at[q, (near, 3)[i]], rx.at[q, i], rx_s.at[q, i], rx_r.at[q, i], dev)
        return rdma(po.at[q, far], rx.at[q, 2], rx_s.at[q, 2], rx_r.at[q, 2], dev2)

    def back_mid(q):
        far = 2 if q == 0 else 1
        back(q, 1).wait_recv()
        add((q, far), rx[q, 1])
        back(q, 2).start()

    def back_end(q, ref):
        back(q, 0).wait_recv()
        back(q, 2).wait_recv()
        ref[...] = (po[q, 0].astype(F32) + rx[q, 0].astype(F32) + rx[q, 2].astype(F32)).astype(BF16)

    def gg_copy(i):
        return rdma(ggs.at[i], gg_ref.at[i], gg_s.at[i], gg_r.at[i], peer(i // 2, i % 2))

    k1, k2, k3 = order[1:]
    own_first()
    own_second()
    acc[...] = jnp.zeros_like(acc)
    lay_weights()
    metas()
    on_line(z, 0, "start")
    own_mid(0)
    own_mid(1)
    wave(1, None)
    far_out(1, 0)
    own_near(0)
    own_near(1)
    load_x(z, 0, True)
    on_line(z, 2, "start")
    gates(z, 0)
    load_g(z, 0, True)
    far_out(1, 1)
    wave(2, None)
    own_far()
    far_out(2, 0)
    hidden_cots(z, 0, True)
    second(0)
    swap(0, 0).start()
    swap(1, 0).start()
    far_mid(1, 0)
    load_x(z, 1, True)
    third(0)
    load_g(z, 1, True)
    gates(z, 1)
    far_mid(1, 1)
    wave(1, 0)
    wave(1, "meta")
    hidden_cots(z, 1, True)
    far_out(2, 1)
    on_line(z, 3, "start")
    second(1)
    swap(0, 1).start()
    swap(1, 1).start()
    for i in range(1, 8):
        gg_copy(i).start()
    gg_ref[0] = ggs[0]
    far_mid(2, 1)
    far_near(1, 1)
    merge(0)
    wave(3, None)
    far_mid(2, 0)
    far_near(1, 0)
    far_out(3, 0)
    on_line(z, 1, "start")
    merge(1)
    third(1)
    far_out(3, 1)
    load_x(k1, 0, False)
    wave(1, 2)
    wave(1, 1)
    far_far(1)
    gates(k1, 0)
    wave(1, 3)
    load_g(k1, 0, False)
    far_near(2, 1)
    far_far(2)
    far_mid(3, 1)
    back(0, 1).start()
    back(0, 0).start()
    hidden_cots(k1, 0, False)
    far_mid(3, 0)
    wave(2, 0)
    wave(2, "meta")
    third(0)
    load_x(k1, 1, False)
    load_g(k1, 1, False)
    far_near(2, 0)
    gates(k1, 1)
    load_x(k2, 0, False)
    back(1, 1).start()
    back(1, 0).start()
    gates(k2, 0)
    wave(2, 1)
    hidden_cots(k1, 1, False)
    third(1)
    load_x(k2, 1, False)
    far_near(3, 0)
    load_g(k2, 0, False)
    far_near(3, 1)
    wave(2, 2)
    hidden_cots(k2, 0, False)
    gates(k2, 1)
    wave(2, 3)
    third(0)
    load_x(k3, 0, False)
    load_g(k2, 1, False)
    far_far(3)
    gates(k3, 0)
    wave(3, 0)
    wave(3, "meta")
    hidden_cots(k2, 1, False)
    third(1)
    wave(3, 1)
    load_x(k3, 1, False)
    back_mid(1)
    back_mid(0)
    wave(3, 2)
    load_g(k3, 0, False)
    gates(k3, 1)
    load_g(k3, 1, False, range(0, 2))
    wave(3, 3)
    hidden_cots(k3, 0, False)
    third(0)
    load_g(k3, 1, False, range(2, 4))
    hidden_cots(k3, 1, False, range(0, 2))
    third(1, range(0, 2))
    hidden_cots(k3, 1, False, range(2, 4))
    third(1, range(2, 4), True)
    back_end(1, tg_ref)
    back_end(0, lay_ref)

    for i in range(3):
        grads_out(i).wait()
    for j in range(4):
        for i in range(6):
            xy(j, i).wait_send()
    for m in range(4):
        sibling(z, m, 0, whole).wait_send()
    for k in (k1, k2, k3):
        for m in range(4):
            sibling(k, m, 0, pa).wait_send()
            sibling(k, m, 1, pb).wait_send()
    for k in order:
        on_line(k, None, "wait_send")
        on_line(k, "meta", "wait_send")
        for m in range(4):
            on_line(k, m, "wait_send")
    for q in range(2):
        for s in range(2):
            swap(q, s).wait_send()
        for i in range(3):
            back(q, i).wait_send()
    for i in range(1, 8):
        gg_copy(i).wait_recv()
        gg_copy(i).wait_send()
        near_meta(i).wait_send()


def finish_kernel(acc_ref, lay_ref, tg_ref, gg_ref, ids_ref, wg_out, lay_out, tg_out, gate_out):
    rows, cols = acc_ref.shape
    h = cols // 6
    for p in range(3):
        for j in range(h // LANES):
            for e in range(2):
                at_row, col = place(h, p, j, e)
                wg_out[pl.ds(at_row, rows, stride=cols // LANES), :] = acc_ref[:, col : col + LANES]
    lay_out[...] = lay_ref[...]
    tg_out[...] = tg_ref[...]

    @pl.when(pl.program_id(0) == 0)
    def _():
        me = lax.axis_index("expert")
        ids = ids_ref[...]
        total = jnp.zeros(ids.shape, F32)
        for i in range(8):
            source = (
                (me // 4 + i // 4) % 2 * 4 + (me // 2 + i // 2) % 2 * 2 + (me + i) % 2
            )
            for e in range(2):
                total = total + jnp.where(ids == 2 * source + e, gg_ref[i, e : e + 1, :], 0.0)
        gate_out[...] = total


def finish(acc, lay, tg, gg, ids):
    rows, cols = acc.shape
    n = 2
    per = cols // LANES
    tall = pl.BlockSpec((rows // n, cols), lambda i: (i, 0))
    wide = pl.BlockSpec((lay.shape[0] // n, lay.shape[1]), lambda i: (i, 0))
    flat = pl.BlockSpec(ids.shape, lambda i: (0, 0))
    return pl.pallas_call(
        finish_kernel,
        grid=(n,),
        out_shape=[
            jax.ShapeDtypeStruct((rows * per, LANES), F32),
            jax.ShapeDtypeStruct(lay.shape, lay.dtype),
            jax.ShapeDtypeStruct(tg.shape, tg.dtype),
            jax.ShapeDtypeStruct(ids.shape, F32),
        ],
        in_specs=[tall, wide, wide, pl.BlockSpec(gg.shape, lambda i: (0, 0, 0)), flat],
        out_specs=[pl.BlockSpec((rows // n * per, LANES), lambda i: (i, 0)), wide, wide, flat],
        compiler_params=pltpu.CompilerParams(vmem_limit_bytes=60 * 1024 * 1024),
    )(acc, lay, tg, gg, ids)


def fused(tokens, expert_ids, gate_probs, expert_weights, out_grad):
    tok, top = expert_ids.shape
    d = tokens.shape[1]
    local_experts, h = expert_weights.shape[2:]
    hh = local_experts * h
    rows = 2 * tok
    ids = expert_ids.T

    w = with_layout_constraint(
        expert_weights.reshape(d, 3, local_experts, h // LANES, LANES),
        Layout(major_to_minor=(0, 1, 3, 2, 4)),
    )
    per = 3 * hh // LANES
    w = jnp.transpose(w, (0, 1, 3, 2, 4)).reshape(d * per, LANES)
    step = 128

    any_ = pl.BlockSpec(memory_space=pl.ANY)
    vmem = pl.BlockSpec(memory_space=pltpu.VMEM)
    dma = pltpu.SemaphoreType.DMA
    lay, tg, gg, acc, _ = pl.pallas_call(
        fused_kernel,
        out_shape=[
            jax.ShapeDtypeStruct((tok, d), BF16),
            jax.ShapeDtypeStruct((tok, d), BF16),
            jax.ShapeDtypeStruct((8, 8, tok), F32),
            jax.ShapeDtypeStruct((d // 4, 3 * hh), F32),
            jax.ShapeDtypeStruct((2, 4, 4, rows, d), BF16),
        ],
        in_specs=[any_, any_, vmem, vmem, any_],
        out_specs=[vmem, vmem, vmem, any_, any_],
        scratch_shapes=[
            pltpu.VMEM((d, 3 * hh), BF16),
            pltpu.VMEM((2, step * per, LANES), BF16),
            pltpu.VMEM((step * per, LANES), F32),
            pltpu.VMEM((2, 4, rows, d), BF16),
            pltpu.VMEM((4, 8, META, 2 * tok), BF16),
            pltpu.VMEM((2, 2, 4 * tok, hh), F32),
            pltpu.VMEM((4 * tok, 3 * hh), BF16),
            pltpu.VMEM((d // 4, 3 * hh), F32),
            pltpu.VMEM((2, 4, tok, d), BF16),
            pltpu.VMEM((2, 4, tok, d), BF16),
            pltpu.VMEM((2, 4, tok, d), BF16),
            pltpu.VMEM((2, 3, tok, d), BF16),
            pltpu.VMEM((8, 8, tok), F32),
            dma((3,)), dma((2,)), dma((2, 4, 2)), dma((3,)),
            dma((4, 6)), dma((4, 6)), dma((4, 2)), dma((4,)),
            dma((4, 4, 2)), dma((4, 4)), dma((4, 4, 2)), dma((4, 4, 2)),
            dma((2, 2)), dma((2, 2)), dma((2, 3)), dma((2, 3)), dma((8,)), dma((8,)),
            dma((8,)), dma((8,)), dma((4, 2)), dma((4,)),
        ],
        compiler_params=pltpu.CompilerParams(
            collective_id=0, has_side_effects=True, vmem_limit_bytes=60 * 1024 * 1024
        ),
    )(tokens, out_grad, ids, gate_probs.T, w)

    wg, lay, tg, gate_grad = finish(acc, lay, tg, gg, ids)
    wg = jnp.transpose(wg.reshape(d // 4, 3, h // LANES, local_experts, LANES), (0, 1, 3, 2, 4))
    wg = with_layout_constraint(wg, Layout(major_to_minor=(0, 1, 3, 2, 4)))
    return lay, tg, gate_grad.T, wg.reshape(d // 4, 3, local_experts, h)


def gather(rows):
    n = lax.axis_size("chip")
    own = [rows] + [
        lax.ppermute(rows, "chip", [(i, i ^ k) for i in range(n)]) for k in range(1, n)
    ]
    own = jnp.concatenate(own, axis=0)
    return jnp.concatenate([own, lax.ppermute(own, "core", SWAP)], axis=0)


def scatter(own, other):
    n = lax.axis_size("chip")
    me = lax.axis_index("chip")
    total = own + lax.ppermute(other, "core", SWAP).astype(F32)
    total = total.astype(other.dtype).reshape((n, -1) + own.shape[1:])
    total = jnp.concatenate(
        [lax.dynamic_index_in_dim(total, me ^ k, 0, keepdims=False) for k in range(n)],
        axis=0,
    )
    return lax.psum_scatter(total, "chip", scatter_dimension=0, tiled=True)


def line_scatter(grad):
    n = lax.axis_size("dp")
    me = lax.axis_index("dp")
    rows = grad.shape[0] // n

    def chunk(i):
        i = jnp.clip(i, 0, n - 1)
        return lax.dynamic_slice_in_dim(grad, i * rows, rows, 0).astype(F32)

    up = down = None
    for t in range(n - 1):
        a = chunk(n - 1 - t + me)
        b = chunk(t - (n - 1) + me)
        if t:
            a = a + up.astype(F32)
            b = b + down.astype(F32)
        up = lax.ppermute(a.astype(BF16), "dp", [(i, i + 1) for i in range(t + 1)])
        down = lax.ppermute(
            b.astype(BF16), "dp", [(i, i - 1) for i in range(n - 1 - t, n)]
        )
    return chunk(me) + up.astype(F32) + down.astype(F32)


def local(tokens, expert_ids, gate_probs, expert_weights, out_grad):
    tok_count, top_count = expert_ids.shape
    d = tokens.shape[1]
    chips = lax.axis_size("chip")
    me = lax.axis_index("chip") * 2 + lax.axis_index("core")
    local_experts, h = expert_weights.shape[2:]
    half = chips * tok_count
    eh = local_experts * h

    x = gather(tokens)
    small = gather(jnp.concatenate([expert_ids.astype(F32), gate_probs], axis=1))
    g = gather(out_grad)
    ids = small[:, :top_count].astype(jnp.int32)
    probs = small[:, top_count:]

    hits = [ids == me * local_experts + i for i in range(local_experts)]
    p = jnp.concatenate(
        [
            jnp.broadcast_to(
                jnp.sum(jnp.where(hit, probs, 0.0), axis=1, keepdims=True), (2 * half, h)
            )
            for hit in hits
        ],
        axis=1,
    )

    w = expert_weights.reshape(d, 3 * eh)
    wgu = w[:, : 2 * eh]
    wd = w[:, 2 * eh :]

    a = dot(x, wgu, 1, 0)
    gate = a[:, :eh]
    up = a[:, eh:]
    s = jax.nn.sigmoid(gate)
    hidden = gate * s * up
    ph = (p * hidden).astype(BF16)
    down_grad = line_scatter(dot(g, ph, 0, 0).astype(BF16))

    u = dot(g, wd, 1, 0)
    hc = p * u
    gc = (hc * up * s * (1.0 + gate * (1.0 - s))).astype(BF16)
    uc = (hc * gate * s).astype(BF16)
    gate_part = line_scatter(dot(x, gc, 0, 0).astype(BF16))
    up_part = line_scatter(dot(x, uc, 0, 0).astype(BF16))

    other = dot(ph[half:], wd, 1, 1).astype(BF16)
    layer_out = scatter(dot(ph[:half], wd, 1, 1), other)

    cots = jnp.concatenate([gc, uc], axis=1)
    other = dot(cots[half:], wgu, 1, 1).astype(BF16)
    token_grad = scatter(dot(cots[:half], wgu, 1, 1), other)

    uh = u * hidden
    ggk = sum(
        jnp.where(hit, jnp.sum(uh[:, i * h : (i + 1) * h], axis=1, keepdims=True), 0.0)
        for i, hit in enumerate(hits)
    )
    gate_grad = scatter(ggk[:half], ggk[half:])

    weight_grad = jnp.stack([gate_part, up_part, down_grad], axis=1)
    weight_grad = weight_grad.reshape(-1, 3, local_experts, h)
    return (layer_out, token_grad, gate_grad, weight_grad)


def solution(mesh):
    experts, groups = mesh.devices.shape
    if (experts, groups) == (8, 4):
        tok = P(("expert", "dp"), None)
        return jax.shard_map(
            fused,
            mesh=mesh,
            in_specs=(tok, tok, tok, P(None, None, "expert", None), tok),
            out_specs=(tok, tok, tok, P("dp", None, "expert", None)),
            check_vma=False,
        )
    split = Mesh(
        mesh.devices.reshape(experts // 2, 2, groups), ("chip", "core", "dp")
    )
    tok = P(("chip", "core", "dp"), None)
    wsp = P(None, None, ("chip", "core"), None)
    return jax.shard_map(
        local,
        mesh=split,
        in_specs=(tok, tok, tok, wsp, tok),
        out_specs=(tok, tok, tok, P("dp", None, ("chip", "core"), None)),
        check_vma=False,
    )
```

```python
import functools
import jax
import jax.numpy as jnp
from jax import lax
from jax.experimental import pallas as pl
from jax.experimental.layout import Layout, with_layout_constraint
from jax.experimental.pallas import tpu as pltpu
from jax.sharding import Mesh, PartitionSpec as P

F32 = jnp.float32
BF16 = jnp.bfloat16
SWAP = [(0, 1), (1, 0)]
META = 16
LANES = 128


def dot(a, b, ca, cb):
    return lax.dot_general(a, b, (((ca,), (cb,)), ((), ())), preferred_element_type=F32)


def place(h, p, j, e):
    return (p * (h // LANES) + j) * 2 + e, (2 * p + e) * h + j * LANES


def fused_kernel(
    tok_ref, og_ref, ids_ref, prob_ref, w_ref,
    lay_ref, tg_ref, gg_ref, acc_ref, buf,
    wv, wst, wf, xg, mb, gu, act, acc, po, ps, pr, rx, ggs,
    loc_sem, w_sem, ld_sem, out_sem,
    xy_s, xy_r, za_s, za_r, zb_s, zb_r, sib_s, sib_r,
    ps_s, ps_r, rx_s, rx_r, gg_s, gg_r, mp_s, mp_r, ml_s, ml_r,
):
    tok, d = tok_ref.shape
    rows = 2 * tok
    hh = wv.shape[1] // 3
    h = hh // 2
    per = 3 * hh // LANES
    step = wf.shape[0] // per
    ch = d // 4
    nt = min(256, hh)
    dt = min(512, d)
    me = lax.axis_index("expert")
    z = lax.axis_index("dp")
    core = me % 2
    xx = (me // 2) % 2
    yy = me // 4

    def peer(m, r):
        return (
            ((yy + m // 2) % 2) * 4 + ((xx + m % 2) % 2) * 2 + (core + r) % 2,
            z,
        )

    xn, yn, sib = peer(1, 0), peer(2, 0), peer(0, 1)
    order = [z, 1 + z % 2, (2 + 3 * z) % 5, 3 - 3 * (z // 2)]

    own_half = tok
    cut_a = rows * 11 // 16 // 16 * 16
    a_half = (cut_a // 2 + 8) // 16 * 16
    h1, h2 = (0, own_half), (own_half, rows - own_half)
    whole, pa, pb = (0, rows), (0, cut_a), (cut_a, rows - cut_a)
    a_rest = cut_a - a_half
    halves = [(h1, h2)] + [((0, a_half), (a_half, a_rest))] * 3

    def rdma(src, dst, ssem, rsem, dev):
        return pltpu.make_async_remote_copy(
            src_ref=src, dst_ref=dst, send_sem=ssem, recv_sem=rsem,
            device_id=dev, device_id_type=pl.DeviceIdType.MESH,
        )

    def at(r, k, m, part):
        return buf.at[r, k, m, pl.ds(part[0], part[1])]

    def xy(j, i):
        k = order[j]
        p1, p2 = halves[j]
        src, dst, part, dev = [
            (0, 1, p1, xn), (0, 1, p2, xn), (0, 2, p2, yn), (0, 2, p1, yn),
            (1, 3, p1, yn), (2, 3, p2, xn),
        ][i]
        rows_out = at(0, k, src, part)
        if j == 0 and i < 4:
            rows_out = tok_ref if part == h1 else og_ref
        return rdma(rows_out, at(0, k, dst, part), xy_s.at[k, i], xy_r.at[k, i], dev)

    def line(k, m, up):
        dev = (me, z + 1) if up else (me, z - 1)
        u = 1 if up else 0
        if m is None:
            return rdma(at(0, k, 0, pa), at(0, k, 0, pa), za_s.at[k, u], za_r.at[k], dev)
        if m == "meta":
            return rdma(mb.at[k], mb.at[k], ml_s.at[k, u], ml_r.at[k], dev)
        return rdma(at(0, k, m, pb), at(0, k, m, pb), zb_s.at[k, m, u], zb_r.at[k, m], dev)

    def on_line(k, m, what):
        @pl.when((k <= z) & (z < 3))
        def _():
            getattr(line(k, m, True), what)()

        @pl.when((k >= z) & (z > 0))
        def _():
            getattr(line(k, m, False), what)()

    def sibling(k, m, i, part):
        return rdma(at(0, k, m, part), at(1, k, m, part), sib_s.at[k, m, i], sib_r.at[k, m, i], sib)

    own = [
        pltpu.make_async_copy(tok_ref, xg.at[0, 0, pl.ds(0, tok)], loc_sem.at[0]),
        pltpu.make_async_copy(og_ref, xg.at[0, 0, pl.ds(tok, tok)], loc_sem.at[1]),
    ]
    held = pltpu.make_async_copy(xg.at[0, 0], buf.at[0, z, 0], loc_sem.at[2])
    for c in own:
        c.start()
    barrier = pltpu.get_barrier_semaphore()
    for i in range(1, 8):
        pl.semaphore_signal(barrier, inc=1, device_id=peer(i // 2, i % 2), device_id_type=pl.DeviceIdType.MESH)

    @pl.when(z > 0)
    def _():
        pl.semaphore_signal(barrier, inc=1, device_id=(me, z - 1), device_id_type=pl.DeviceIdType.MESH)

    @pl.when(z < 3)
    def _():
        pl.semaphore_signal(barrier, inc=1, device_id=(me, z + 1), device_id_type=pl.DeviceIdType.MESH)

    named = lax.broadcasted_iota(jnp.int32, (META, tok), 0)
    prob = jnp.zeros((META, tok), F32)
    for i in range(ids_ref.shape[0]):
        prob = prob + jnp.where(named == ids_ref[i : i + 1, :], prob_ref[i : i + 1, :], 0.0)
    high = prob.astype(BF16)
    mb[z, 0, :, :tok] = high
    mb[z, 0, :, tok:] = (prob - high.astype(F32)).astype(BF16)
    for c in own:
        c.wait()
    held.start()
    pl.semaphore_wait(barrier, 8 + (z + 1) // 2 % 2)

    def own_first():
        xy(0, 0).start()
        xy(0, 2).start()
        for i in range(1, 8):
            near_meta(i).start()
        held.wait()
        on_line(z, None, "start")

    def own_second():
        xy(0, 1).start()
        xy(0, 3).start()
        sibling(z, 0, 0, whole).start()

    def own_mid(i):
        xy(0, 2 * i).wait_recv()
        xy(0, 4 + i).start()

    def own_near(i):
        xy(0, 1 + 2 * i).wait_recv()
        sibling(z, 1 + i, 0, whole).start()

    def own_far():
        xy(0, 4).wait_recv()
        xy(0, 5).wait_recv()
        sibling(z, 3, 0, whole).start()

    def near_meta(i):
        return rdma(mb.at[z, 0], mb.at[z, i], mp_s.at[i], mp_r.at[i], peer(i // 2, i % 2))

    def metas():
        for i in range(1, 8):
            near_meta(i).wait_recv()
        on_line(z, "meta", "start")

    def wave(n, m):
        @pl.when(z + n <= 3)
        def _():
            take(z + n, m)

            @pl.when(z > 0)
            def _():
                line(z + n, m, False).start()

        @pl.when(z - n >= 0)
        def _():
            take(z - n, m)

            @pl.when(z < 3)
            def _():
                line(z - n, m, True).start()

    def take(k, m):
        line(k, m, True).wait_recv()
        if m is None:
            sibling(k, 0, 0, pa).start()
        elif m != "meta":
            sibling(k, m, 1, pb).start()

    def far_out(j, i):
        xy(j, i).start()
        xy(j, (2, 3)[i]).start()

    def far_mid(j, i):
        xy(j, 2 * i).wait_recv()
        xy(j, 4 + i).start()

    def far_near(j, i):
        xy(j, 1 + 2 * i).wait_recv()
        sibling(order[j], 1 + i, 0, pa).start()

    def far_far(j):
        xy(j, 4).wait_recv()
        xy(j, 5).wait_recv()
        sibling(order[j], 3, 0, pa).start()

    def raw(c):
        return pltpu.make_async_copy(
            w_ref.at[pl.ds(pl.multiple_of(c * step * per, step * per), step * per)],
            wst.at[c % 2], w_sem.at[c % 2],
        )

    def lay_weights():
        n = d // step
        raw(0).start()

        def chunk(c, carry):
            @pl.when(c + 1 < n)
            def _():
                raw(c + 1).start()

            raw(c).wait()
            wf[...] = wst[c % 2].astype(F32)
            to = pl.ds(pl.multiple_of(c * step, step), step)
            for p in range(3):
                for j in range(h // LANES):
                    for e in range(2):
                        at_row, col = place(h, p, j, e)
                        wv[to, col : col + LANES] = wf[pl.ds(at_row, step, stride=per), :].astype(BF16)
            return carry

        lax.fori_loop(0, n, chunk, 0)

    def load(k, s, i, what, blocks=range(4)):
        for b in blocks:
            part = pl.ds(i * tok, tok)
            c = pltpu.make_async_copy(
                buf.at[b % 2, k, 2 * s + b // 2, part], xg.at[s, b, part], ld_sem.at[s, b, i]
            )
            getattr(c, what)()

    def load_x(k, s, mine):
        for m in (2 * s, 2 * s + 1):
            sibling(k, m, 0, whole if mine else pa).wait_recv()
        load(k, s, 0, "start")

    def load_g(k, s, mine, blocks=range(4)):
        if not mine:
            for b in blocks[::2]:
                sibling(k, 2 * s + b // 2, 1, pb).wait_recv()
        load(k, s, 1, "start", blocks)

    def gates(k, s):
        load(k, s, 0, "wait")

        def tile(n, carry):
            c0 = pl.multiple_of(n * nt, nt)
            xs = xg[s, :, 0:tok, :].reshape(4 * tok, d)
            for i in range(2):
                gu[s, i, :, pl.ds(c0, nt)] = dot(xs, wv[:, pl.ds(i * hh + c0, nt)], 1, 0)
            return carry

        lax.fori_loop(0, hh // nt, tile, 0)

    def hidden_cots(k, s, mine, blocks=range(4)):
        load(k, s, 1, "wait", blocks)
        b0, b1, n_rows = blocks[0], blocks[-1] + 1, len(blocks) * tok
        span = slice(b0 * tok, b1 * tok)

        def tile(n, gg):
            c0 = pl.multiple_of(n * nt, nt)
            gs = xg[s, b0:b1, tok:, :].reshape(n_rows, d)
            u = dot(gs, wv[:, pl.ds(2 * hh + c0, nt)], 1, 0)
            gate = gu[s, 0, span, pl.ds(c0, nt)]
            up = gu[s, 1, span, pl.ds(c0, nt)]
            col = c0 + lax.broadcasted_iota(jnp.int32, (2 * META, nt), 1)
            row = lax.broadcasted_iota(jnp.int32, (2 * META, nt), 0) % META
            sel = (row == 2 * me + (col >= h).astype(jnp.int32)).astype(F32).astype(BF16)
            shares = []
            for b in blocks:
                both = jnp.concatenate(
                    [mb[k, 4 * s + b, :, :tok], mb[k, 4 * s + b, :, tok:]], axis=0
                )
                shares.append(dot(both, sel, 0, 0))
            p = jnp.concatenate(shares, axis=0)
            sig = jax.nn.sigmoid(gate)
            silu = gate * sig
            hidden = silu * up
            hc = p * u
            act[span, pl.ds(c0, nt)] = (hc * up * (sig + silu * (1.0 - sig))).astype(BF16)
            act[span, pl.ds(hh + c0, nt)] = (hc * silu).astype(BF16)
            act[span, pl.ds(2 * hh + c0, nt)] = (p * hidden).astype(BF16)
            if mine:
                uh = u * hidden
                hi = uh.astype(BF16)
                lo = (uh - hi.astype(F32)).astype(BF16)
                own_row = lax.broadcasted_iota(jnp.int32, (8, nt), 0)
                own_col = c0 + lax.broadcasted_iota(jnp.int32, (8, nt), 1)
                pick = (own_row == (own_col >= h).astype(jnp.int32)).astype(F32).astype(BF16)
                gg = gg + dot(pick, hi, 1, 1) + dot(pick, lo, 1, 1)
            return gg

        start = jnp.zeros((8, 4 * tok), F32)
        gg = lax.fori_loop(0, hh // nt, tile, start)
        if mine:
            for b in range(4):
                ggs[4 * s + b] = gg[:, b * tok : (b + 1) * tok]

    def third(s, blocks=range(4), last=False):
        x0 = pl.multiple_of(z * ch, ch)
        b0, b1, n_rows = blocks[0], blocks[-1] + 1, len(blocks) * tok
        span = slice(b0 * tok, b1 * tok)
        cuts = ((0, hh), (hh, hh), (2 * hh, hh)) if last else ((0, 2 * hh), (2 * hh, hh))
        for i, (c0, width) in enumerate(cuts):
            top = tok if c0 == 2 * hh else 0
            rows_in = xg[s, b0:b1, top : top + tok, pl.ds(x0, ch)].reshape(n_rows, ch)
            acc[:, c0 : c0 + width] += dot(rows_in, act[span, c0 : c0 + width], 0, 0)
            if last:
                grads_out(i).start()

    def grads_out(i):
        part = pl.ds(i * hh, hh)
        return pltpu.make_async_copy(acc.at[:, part], acc_ref.at[:, part], out_sem.at[i])

    def second(s):
        def tile(n, carry):
            r0 = pl.multiple_of(n * dt, dt)
            out = dot(act[:, 2 * hh :], wv[pl.ds(r0, dt), 2 * hh :], 1, 1).astype(BF16)
            tg = dot(act[:, : 2 * hh], wv[pl.ds(r0, dt), : 2 * hh], 1, 1).astype(BF16)
            for mi in range(2):
                for q, v in ((0, out), (1, tg)):
                    b = 2 * mi * tok
                    po[q, 2 * s + mi, :, pl.ds(r0, dt)] = v[b : b + tok]
                    ps[q, 2 * s + mi, :, pl.ds(r0, dt)] = v[b + tok : b + 2 * tok]
            return carry

        lax.fori_loop(0, d // dt, tile, 0)

    def swap(q, s):
        part = pl.ds(2 * s, 2)
        return rdma(ps.at[q, part], pr.at[q, part], ps_s.at[q, s], ps_r.at[q, s], sib)

    def add(i, j):
        po[i] = (po[i].astype(F32) + j.astype(F32)).astype(BF16)

    def merge(s):
        for q in range(2):
            swap(q, s).wait_recv()
            for m in (2 * s, 2 * s + 1):
                add((q, m), pr[q, m])

    def back(q, i):
        near, far = (1, 2) if q == 0 else (2, 1)
        dev, dev2 = (xn, yn) if q == 0 else (yn, xn)
        if i < 2:
            return rdma(po.at[q, (near, 3)[i]], rx.at[q, i], rx_s.at[q, i], rx_r.at[q, i], dev)
        return rdma(po.at[q, far], rx.at[q, 2], rx_s.at[q, 2], rx_r.at[q, 2], dev2)

    def back_mid(q):
        far = 2 if q == 0 else 1
        back(q, 1).wait_recv()
        add((q, far), rx[q, 1])
        back(q, 2).start()

    def back_end(q, ref):
        back(q, 0).wait_recv()
        back(q, 2).wait_recv()
        ref[...] = (po[q, 0].astype(F32) + rx[q, 0].astype(F32) + rx[q, 2].astype(F32)).astype(BF16)

    def gg_copy(i):
        return rdma(ggs.at[i], gg_ref.at[i], gg_s.at[i], gg_r.at[i], peer(i // 2, i % 2))

    k1, k2, k3 = order[1:]
    own_first()
    acc[...] = jnp.zeros_like(acc)
    lay_weights()
    own_second()
    wave(1, None)
    far_out(1, 0)
    own_mid(0)
    own_near(0)
    metas()
    on_line(z, 0, "start")
    own_mid(1)
    far_out(1, 1)
    wave(2, None)
    load_x(z, 0, True)
    gates(z, 0)
    far_mid(1, 0)
    own_near(1)
    far_out(2, 0)
    load_g(z, 0, True)
    own_far()
    hidden_cots(z, 0, True)
    load_x(z, 1, True)
    far_mid(1, 1)
    far_near(1, 0)
    on_line(z, 1, "start")
    second(0)
    swap(0, 0).start()
    swap(1, 0).start()
    load_g(z, 1, True)
    wave(3, None)
    on_line(z, 3, "start")
    far_out(3, 0)
    gates(z, 1)
    wave(1, 0)
    wave(1, "meta")
    third(0)
    far_out(3, 1)
    far_mid(2, 0)
    far_mid(2, 1)
    hidden_cots(z, 1, True)
    load_x(k1, 0, False)
    second(1)
    swap(0, 1).start()
    swap(1, 1).start()
    for i in range(1, 8):
        gg_copy(i).start()
    gg_ref[0] = ggs[0]
    merge(0)
    far_out(2, 1)
    on_line(z, 2, "start")
    wave(1, 1)
    gates(k1, 0)
    far_far(1)
    merge(1)
    wave(1, 3)
    third(1)
    far_mid(3, 0)
    far_near(1, 1)
    load_g(k1, 0, False)
    far_mid(3, 1)
    far_far(2)
    wave(1, 2)
    hidden_cots(k1, 0, False)
    far_near(2, 0)
    back(0, 1).start()
    back(0, 0).start()
    back(1, 1).start()
    back(1, 0).start()
    wave(2, 1)
    far_near(3, 1)
    load_x(k1, 1, False)
    gates(k1, 1)
    third(0)
    load_g(k1, 1, False)
    load_x(k2, 0, False)
    hidden_cots(k1, 1, False)
    wave(2, 0)
    wave(2, "meta")
    far_near(2, 1)
    gates(k2, 0)
    load_g(k2, 0, False)
    third(1)
    far_near(3, 0)
    load_x(k2, 1, False)
    hidden_cots(k2, 0, False)
    third(0)
    far_far(3)
    wave(2, 2)
    load_x(k3, 0, False)
    gates(k2, 1)
    wave(2, 3)
    gates(k3, 0)
    load_g(k2, 1, False)
    wave(3, 1)
    back_mid(0)
    wave(3, 0)
    wave(3, "meta")
    back_mid(1)
    hidden_cots(k2, 1, False)
    load_g(k3, 0, False)
    third(1)
    load_x(k3, 1, False)
    hidden_cots(k3, 0, False)
    wave(3, 2)
    gates(k3, 1)
    load_g(k3, 1, False, range(0, 2))
    wave(3, 3)
    third(0)
    back_end(0, lay_ref)
    hidden_cots(k3, 1, False, range(0, 2))
    load_g(k3, 1, False, range(2, 4))
    third(1, range(0, 2))
    back_end(1, tg_ref)
    hidden_cots(k3, 1, False, range(2, 4))
    third(1, range(2, 4), True)

    for i in range(3):
        grads_out(i).wait()
    for j in range(4):
        for i in range(6):
            xy(j, i).wait_send()
    for m in range(4):
        sibling(z, m, 0, whole).wait_send()
    for k in (k1, k2, k3):
        for m in range(4):
            sibling(k, m, 0, pa).wait_send()
            sibling(k, m, 1, pb).wait_send()
    for k in order:
        on_line(k, None, "wait_send")
        on_line(k, "meta", "wait_send")
        for m in range(4):
            on_line(k, m, "wait_send")
    for q in range(2):
        for s in range(2):
            swap(q, s).wait_send()
        for i in range(3):
            back(q, i).wait_send()
    for i in range(1, 8):
        gg_copy(i).wait_recv()
        gg_copy(i).wait_send()
        near_meta(i).wait_send()


def finish_kernel(acc_ref, lay_ref, tg_ref, gg_ref, ids_ref, wg_out, lay_out, tg_out, gate_out):
    rows, cols = acc_ref.shape
    h = cols // 6
    for p in range(3):
        for j in range(h // LANES):
            for e in range(2):
                at_row, col = place(h, p, j, e)
                wg_out[pl.ds(at_row, rows, stride=cols // LANES), :] = acc_ref[:, col : col + LANES]
    lay_out[...] = lay_ref[...]
    tg_out[...] = tg_ref[...]

    @pl.when(pl.program_id(0) == 0)
    def _():
        me = lax.axis_index("expert")
        ids = ids_ref[...]
        total = jnp.zeros(ids.shape, F32)
        for i in range(8):
            source = (
                (me // 4 + i // 4) % 2 * 4 + (me // 2 + i // 2) % 2 * 2 + (me + i) % 2
            )
            for e in range(2):
                total = total + jnp.where(ids == 2 * source + e, gg_ref[i, e : e + 1, :], 0.0)
        gate_out[...] = total


def finish(acc, lay, tg, gg, ids):
    rows, cols = acc.shape
    n = 2
    per = cols // LANES
    tall = pl.BlockSpec((rows // n, cols), lambda i: (i, 0))
    wide = pl.BlockSpec((lay.shape[0] // n, lay.shape[1]), lambda i: (i, 0))
    flat = pl.BlockSpec(ids.shape, lambda i: (0, 0))
    return pl.pallas_call(
        finish_kernel,
        grid=(n,),
        out_shape=[
            jax.ShapeDtypeStruct((rows * per, LANES), F32),
            jax.ShapeDtypeStruct(lay.shape, lay.dtype),
            jax.ShapeDtypeStruct(tg.shape, tg.dtype),
            jax.ShapeDtypeStruct(ids.shape, F32),
        ],
        in_specs=[tall, wide, wide, pl.BlockSpec(gg.shape, lambda i: (0, 0, 0)), flat],
        out_specs=[pl.BlockSpec((rows // n * per, LANES), lambda i: (i, 0)), wide, wide, flat],
        compiler_params=pltpu.CompilerParams(vmem_limit_bytes=60 * 1024 * 1024),
    )(acc, lay, tg, gg, ids)


def fused(tokens, expert_ids, gate_probs, expert_weights, out_grad):
    tok, top = expert_ids.shape
    d = tokens.shape[1]
    local_experts, h = expert_weights.shape[2:]
    hh = local_experts * h
    rows = 2 * tok
    ids = expert_ids.T

    w = with_layout_constraint(
        expert_weights.reshape(d, 3, local_experts, h // LANES, LANES),
        Layout(major_to_minor=(0, 1, 3, 2, 4)),
    )
    per = 3 * hh // LANES
    w = jnp.transpose(w, (0, 1, 3, 2, 4)).reshape(d * per, LANES)
    step = 128

    any_ = pl.BlockSpec(memory_space=pl.ANY)
    vmem = pl.BlockSpec(memory_space=pltpu.VMEM)
    dma = pltpu.SemaphoreType.DMA
    lay, tg, gg, acc, _ = pl.pallas_call(
        fused_kernel,
        out_shape=[
            jax.ShapeDtypeStruct((tok, d), BF16),
            jax.ShapeDtypeStruct((tok, d), BF16),
            jax.ShapeDtypeStruct((8, 8, tok), F32),
            jax.ShapeDtypeStruct((d // 4, 3 * hh), F32),
            jax.ShapeDtypeStruct((2, 4, 4, rows, d), BF16),
        ],
        in_specs=[any_, any_, vmem, vmem, any_],
        out_specs=[vmem, vmem, vmem, any_, any_],
        scratch_shapes=[
            pltpu.VMEM((d, 3 * hh), BF16),
            pltpu.VMEM((2, step * per, LANES), BF16),
            pltpu.VMEM((step * per, LANES), F32),
            pltpu.VMEM((2, 4, rows, d), BF16),
            pltpu.VMEM((4, 8, META, 2 * tok), BF16),
            pltpu.VMEM((2, 2, 4 * tok, hh), F32),
            pltpu.VMEM((4 * tok, 3 * hh), BF16),
            pltpu.VMEM((d // 4, 3 * hh), F32),
            pltpu.VMEM((2, 4, tok, d), BF16),
            pltpu.VMEM((2, 4, tok, d), BF16),
            pltpu.VMEM((2, 4, tok, d), BF16),
            pltpu.VMEM((2, 3, tok, d), BF16),
            pltpu.VMEM((8, 8, tok), F32),
            dma((3,)), dma((2,)), dma((2, 4, 2)), dma((3,)),
            dma((4, 6)), dma((4, 6)), dma((4, 2)), dma((4,)),
            dma((4, 4, 2)), dma((4, 4)), dma((4, 4, 2)), dma((4, 4, 2)),
            dma((2, 2)), dma((2, 2)), dma((2, 3)), dma((2, 3)), dma((8,)), dma((8,)),
            dma((8,)), dma((8,)), dma((4, 2)), dma((4,)),
        ],
        compiler_params=pltpu.CompilerParams(
            collective_id=0, has_side_effects=True, vmem_limit_bytes=60 * 1024 * 1024
        ),
    )(tokens, out_grad, ids, gate_probs.T, w)

    wg, lay, tg, gate_grad = finish(acc, lay, tg, gg, ids)
    wg = jnp.transpose(wg.reshape(d // 4, 3, h // LANES, local_experts, LANES), (0, 1, 3, 2, 4))
    wg = with_layout_constraint(wg, Layout(major_to_minor=(0, 1, 3, 2, 4)))
    return lay, tg, gate_grad.T, wg.reshape(d // 4, 3, local_experts, h)


def gather(rows):
    n = lax.axis_size("chip")
    own = [rows] + [
        lax.ppermute(rows, "chip", [(i, i ^ k) for i in range(n)]) for k in range(1, n)
    ]
    own = jnp.concatenate(own, axis=0)
    return jnp.concatenate([own, lax.ppermute(own, "core", SWAP)], axis=0)


def scatter(own, other):
    n = lax.axis_size("chip")
    me = lax.axis_index("chip")
    total = own + lax.ppermute(other, "core", SWAP).astype(F32)
    total = total.astype(other.dtype).reshape((n, -1) + own.shape[1:])
    total = jnp.concatenate(
        [lax.dynamic_index_in_dim(total, me ^ k, 0, keepdims=False) for k in range(n)],
        axis=0,
    )
    return lax.psum_scatter(total, "chip", scatter_dimension=0, tiled=True)


def line_scatter(grad):
    n = lax.axis_size("dp")
    me = lax.axis_index("dp")
    rows = grad.shape[0] // n

    def chunk(i):
        i = jnp.clip(i, 0, n - 1)
        return lax.dynamic_slice_in_dim(grad, i * rows, rows, 0).astype(F32)

    up = down = None
    for t in range(n - 1):
        a = chunk(n - 1 - t + me)
        b = chunk(t - (n - 1) + me)
        if t:
            a = a + up.astype(F32)
            b = b + down.astype(F32)
        up = lax.ppermute(a.astype(BF16), "dp", [(i, i + 1) for i in range(t + 1)])
        down = lax.ppermute(
            b.astype(BF16), "dp", [(i, i - 1) for i in range(n - 1 - t, n)]
        )
    return chunk(me) + up.astype(F32) + down.astype(F32)


def local(tokens, expert_ids, gate_probs, expert_weights, out_grad):
    tok_count, top_count = expert_ids.shape
    d = tokens.shape[1]
    chips = lax.axis_size("chip")
    me = lax.axis_index("chip") * 2 + lax.axis_index("core")
    local_experts, h = expert_weights.shape[2:]
    half = chips * tok_count
    eh = local_experts * h

    x = gather(tokens)
    small = gather(jnp.concatenate([expert_ids.astype(F32), gate_probs], axis=1))
    g = gather(out_grad)
    ids = small[:, :top_count].astype(jnp.int32)
    probs = small[:, top_count:]

    hits = [ids == me * local_experts + i for i in range(local_experts)]
    p = jnp.concatenate(
        [
            jnp.broadcast_to(
                jnp.sum(jnp.where(hit, probs, 0.0), axis=1, keepdims=True), (2 * half, h)
            )
            for hit in hits
        ],
        axis=1,
    )

    w = expert_weights.reshape(d, 3 * eh)
    wgu = w[:, : 2 * eh]
    wd = w[:, 2 * eh :]

    a = dot(x, wgu, 1, 0)
    gate = a[:, :eh]
    up = a[:, eh:]
    s = jax.nn.sigmoid(gate)
    hidden = gate * s * up
    ph = (p * hidden).astype(BF16)
    down_grad = line_scatter(dot(g, ph, 0, 0).astype(BF16))

    u = dot(g, wd, 1, 0)
    hc = p * u
    gc = (hc * up * s * (1.0 + gate * (1.0 - s))).astype(BF16)
    uc = (hc * gate * s).astype(BF16)
    gate_part = line_scatter(dot(x, gc, 0, 0).astype(BF16))
    up_part = line_scatter(dot(x, uc, 0, 0).astype(BF16))

    other = dot(ph[half:], wd, 1, 1).astype(BF16)
    layer_out = scatter(dot(ph[:half], wd, 1, 1), other)

    cots = jnp.concatenate([gc, uc], axis=1)
    other = dot(cots[half:], wgu, 1, 1).astype(BF16)
    token_grad = scatter(dot(cots[:half], wgu, 1, 1), other)

    uh = u * hidden
    ggk = sum(
        jnp.where(hit, jnp.sum(uh[:, i * h : (i + 1) * h], axis=1, keepdims=True), 0.0)
        for i, hit in enumerate(hits)
    )
    gate_grad = scatter(ggk[:half], ggk[half:])

    weight_grad = jnp.stack([gate_part, up_part, down_grad], axis=1)
    weight_grad = weight_grad.reshape(-1, 3, local_experts, h)
    return (layer_out, token_grad, gate_grad, weight_grad)


def solution(mesh):
    experts, groups = mesh.devices.shape
    if (experts, groups) == (8, 4):
        tok = P(("expert", "dp"), None)
        return jax.shard_map(
            fused,
            mesh=mesh,
            in_specs=(tok, tok, tok, P(None, None, "expert", None), tok),
            out_specs=(tok, tok, tok, P("dp", None, "expert", None)),
            check_vma=False,
        )
    split = Mesh(
        mesh.devices.reshape(experts // 2, 2, groups), ("chip", "core", "dp")
    )
    tok = P(("chip", "core", "dp"), None)
    wsp = P(None, None, ("chip", "core"), None)
    return jax.shard_map(
        local,
        mesh=split,
        in_specs=(tok, tok, tok, wsp, tok),
        out_specs=(tok, tok, tok, P("dp", None, ("chip", "core"), None)),
        check_vma=False,
    )
```
